32 devices in a mesh: inner: 4 (over y, core), outer: 8 (over z, x).
Axes of the slice: x: 2, y: 2, z: 4, core: 2. Of those that a mesh axis runs over, the one named last changes fastest.
Arguments:
- layer_input: bfloat16 [4096, 2048], P(('inner', 'outer')), may hold values from -6 to 6
- segments: int32 [4096], P(('inner', 'outer')), may hold values from 0 to 11, as said below
- positions: int32 [4096], P(('inner', 'outer')), may hold values from 0 to 511, as said below
- query_key_value_weight: bfloat16 [2048, 1920], P(('inner', 'outer')), may hold values from -0.125 to 0.125
- w_out: bfloat16 [2048, 1280], P(('inner', 'outer')), may hold values from -2.5 to 2.5
- w_gate: bfloat16 [2048, 5120], P(('inner', 'outer')), may hold values from -0.125 to 0.125
- w_up: bfloat16 [2048, 5120], P(('inner', 'outer')), may hold values from -0.125 to 0.125
- w_down: bfloat16 [2048, 5120], P(('inner', 'outer')), may hold values from -0.078125 to 0.078125
- g_attn: float32 [2048], replicated, may hold values from 0.1 to 1.9
- g_ffn: float32 [2048], replicated, may hold values from 0.1 to 1.9
- g_query: float32 [64], replicated, may hold values from 0.1 to 1.9
- g_key: float32 [64], replicated, may hold values from 0.1 to 1.9
- cotangent: bfloat16 [4096, 2048], P(('inner', 'outer')), may hold values from -6 to 6
Outputs:
- result: bfloat16 [4096, 2048], P(('inner', 'outer'))
- input_grad: bfloat16 [4096, 2048], P(('inner', 'outer'))
- w_qkv_grad: float32 [2048, 1920], P(('inner', 'outer'))
- w_out_grad: float32 [2048, 1280], P(('inner', 'outer'))
- w_gate_grad: float32 [2048, 5120], P(('inner', 'outer'))
- w_up_grad: float32 [2048, 5120], P(('inner', 'outer'))
- w_down_grad: float32 [2048, 5120], P(('inner', 'outer'))
- g_attn_grad: float32 [2048], replicated
- g_ffn_grad: float32 [2048], replicated
- g_query_grad: float32 [64], replicated
- g_key_grad: float32 [64], replicated
The draws below stay inside these ranges and needn't reach their ends.
Inputs may be any that keep to these rules, and one draw needn't show every extreme that they name: `segments`: segment numbers never fall along the tokens; each packed sequence of 1024 tokens holds exactly three documents, numbered on from the previous sequence's: a first one of 1 to 511 tokens, then one of 512 tokens, then the rest. `positions`: A token's position is its index in its document: 0 at each segment's first token, rising by one per token.
All inputs are finite; a program needn't handle non-finite values.
Results may differ from the reference program's by a relative error of at most 0.015.
Values may be sent and summed in bfloat16 or wider, within the bound.
No kernel may reach another device: no remote copies, remote signals or barrier semaphores. Data moves between devices by JAX's collectives and lax.ppermute only.
A program may use at most 384 MiB of HBM per device.

```python
import jax
import jax.numpy as jnp
from jax import lax

MODEL_DIM = 2048
FF = 5120
QUERY_HEADS = 20
KEY_VALUE_HEADS = 5
HEAD_DIM = 64
TOK_DEV = 128
PACKED_LENGTH = 1024
PACKED_SEQUENCES = 4
TOTAL_TOKENS = 4096


def document_layout(key):
    seq_count = TOTAL_TOKENS // PACKED_LENGTH
    half_len = PACKED_LENGTH // 2
    block_count = half_len // TOK_DEV
    whole_blocks = jax.random.randint(jax.random.fold_in(key, 11), (seq_count, 1), 0, block_count)
    remainder = jax.random.randint(jax.random.fold_in(key, 12), (seq_count, 1), 1, TOK_DEV)
    first_len = (whole_blocks * TOK_DEV + remainder).astype(jnp.int32)
    local_index = jnp.arange(PACKED_LENGTH, dtype=jnp.int32)[None, :]
    doc_local = jnp.where(local_index < first_len, 0, jnp.where(local_index < first_len + half_len, 1, 2))
    doc_start = jnp.where(local_index < first_len, 0, jnp.where(local_index < first_len + half_len, first_len, first_len + half_len))
    seq_number = jnp.arange(seq_count, dtype=jnp.int32)[:, None]
    segment_ids = (seq_number * 3 + doc_local).astype(jnp.int32).reshape(TOTAL_TOKENS)
    position_ids = (local_index - doc_start).astype(jnp.int32).reshape(TOTAL_TOKENS)
    return (segment_ids, position_ids)


def draw_segments(key, part):
    return document_layout(key)[0]


def draw_positions(key, part):
    return document_layout(key)[1]


def block_levels(rng, shape, cuts, low, high):
    def one(dim, blocks):
        heights = jax.random.uniform(jax.random.fold_in(jax.random.fold_in(rng, 6), dim), (blocks,), jnp.float32, low / len(cuts), high / len(cuts))
        return jnp.repeat(jnp.exp(heights), shape[dim] // blocks).reshape((-1,) + (1,) * (len(shape) - dim - 1))

    factor_of = one(*cuts[0])
    for cut in cuts[1:]:
        factor_of = factor_of * one(*cut)
    return factor_of


def gaussian(key, extent, spread, limit, pieces=(), kind=jnp.bfloat16):
    values = jax.random.normal(key, extent, jnp.float32) * spread
    if len(pieces) > 0:
        values = block_levels(key, extent, pieces, -0.22, 0.18) * values
    return jnp.clip(values, min=-limit, max=limit).astype(kind)


def setup_inputs(seed: int = 0) -> dict:
    key_of = jax.random.split(jax.random.key(seed), 14)
    layer_input = gaussian(key_of[0], (TOTAL_TOKENS, MODEL_DIM), 1.0, 6.0, ((0, 32),))
    segments = draw_segments(jax.random.fold_in(key_of[13], 71), 0)
    positions = draw_positions(jax.random.fold_in(key_of[13], 71), 0)
    query_key_value_weight = gaussian(key_of[3], (MODEL_DIM, (QUERY_HEADS + 2 * KEY_VALUE_HEADS) * HEAD_DIM), MODEL_DIM ** -0.5, 0.125, ((0, 32),))
    w_out = gaussian(key_of[4], (MODEL_DIM, QUERY_HEADS * HEAD_DIM), (max(QUERY_HEADS * HEAD_DIM // 256, 1)) ** -0.5, 2.5, ((0, 32),))
    w_gate = gaussian(key_of[5], (MODEL_DIM, FF), MODEL_DIM ** -0.5, 0.125, ((0, 32),))
    w_up = gaussian(key_of[6], (MODEL_DIM, FF), MODEL_DIM ** -0.5, 0.125, ((0, 32),))
    w_down = gaussian(key_of[7], (MODEL_DIM, FF), FF ** -0.5, 0.078125, ((0, 32),))
    g_attn = jnp.clip(1.0 + 0.18 * jax.random.normal(key_of[8], (MODEL_DIM,), jnp.float32), 0.1, 1.9)
    g_ffn = jnp.clip(1.0 + 0.18 * jax.random.normal(key_of[9], (MODEL_DIM,), jnp.float32), 0.1, 1.9)
    g_query = jnp.clip(1.0 + 0.18 * jax.random.normal(key_of[10], (HEAD_DIM,), jnp.float32), 0.1, 1.9)
    g_key = jnp.clip(1.0 + 0.18 * jax.random.normal(key_of[11], (HEAD_DIM,), jnp.float32), 0.1, 1.9)
    cotangent = gaussian(key_of[12], (TOTAL_TOKENS, MODEL_DIM), 1.0, 6.0, ((0, 32),))
    return dict(layer_input=layer_input, segments=segments, positions=positions, query_key_value_weight=query_key_value_weight, w_out=w_out, w_gate=w_gate, w_up=w_up, w_down=w_down, g_attn=g_attn, g_ffn=g_ffn, g_query=g_query, g_key=g_key, cotangent=cotangent)


@jax.custom_vjp
def low(v):
    return lax.optimization_barrier(v.astype(jnp.bfloat16)).astype(jnp.float32)

@jax.custom_vjp
def low_back(v):
    return v

def low_keep(v):
    return (low(v), None)

def low_pass(kept, grad):
    return (grad,)

def back_keep(v):
    return (v, None)

def back_low(kept, grad):
    return (low(grad),)
low.defvjp(low_keep, low_pass)
low_back.defvjp(back_keep, back_low)
norm_eps = 1e-06

def high_dot(left, right):
    return jnp.dot(left, right, precision=lax.Precision.HIGHEST)

def row_scale(values):
    return lax.rsqrt(lax.optimization_barrier(jnp.mean(values * values, axis=-1, keepdims=True)) + norm_eps)

def rotary_tables(positions):
    half_size = HEAD_DIM // 2
    frequency = 10000.0 ** (-jnp.arange(half_size, dtype=jnp.float32) / half_size)
    angles = positions.astype(jnp.float32)[:, None] * frequency[None, :]
    angles = jnp.concatenate([angles, angles], axis=-1)
    return (jnp.cos(angles)[:, None, :], jnp.sin(angles)[:, None, :])

def rotate(values, cosine, sine_part):
    half_size = values.shape[-1] // 2
    turned = jnp.concatenate([-values[..., half_size:], values[..., :half_size]], axis=-1)
    return values * cosine + turned * sine_part

def one_head(operands, allowed):
    query_head, key_head, value_head = operands
    scores = low_back(jnp.dot(query_head, key_head.T, precision=lax.Precision.HIGHEST))
    scores = jnp.where(allowed, scores, -1e+30)
    row_max = lax.optimization_barrier(jnp.max(scores, axis=-1, keepdims=True))
    exponent = jnp.exp(scores - row_max)
    probabilities = exponent / lax.optimization_barrier(jnp.sum(exponent, axis=-1, keepdims=True))
    return jnp.dot(low(probabilities), value_head, precision=lax.Precision.HIGHEST)

def sequence_attention(operands):
    query_seq, key_seq, value_seq, segment_seq = operands
    token_index = jnp.arange(segment_seq.shape[0])
    allowed = (segment_seq[:, None] == segment_seq[None, :]) & (token_index[None, :] <= token_index[:, None])
    queries_per_group = QUERY_HEADS // KEY_VALUE_HEADS
    key_rep = jnp.repeat(key_seq, queries_per_group, axis=0)
    value_rep = jnp.repeat(value_seq, queries_per_group, axis=0)
    head_fn = jax.checkpoint(lambda ops: one_head(ops, allowed))
    return lax.map(head_fn, (query_seq, key_rep, value_rep))

def reference(layer_input, segments, positions, query_key_value_weight, w_out, w_gate, w_up, w_down, g_attn, g_ffn, g_query, g_key, cotangent):
    query_columns = QUERY_HEADS * HEAD_DIM
    key_value_columns = KEY_VALUE_HEADS * HEAD_DIM
    cosine, sine_part = rotary_tables(positions)

    def forward(inputs, wq, wo, wg, wu, wd, gain_attn, gain_ffn, gain_query, gain_key):
        normed_in = low(inputs * row_scale(inputs) * gain_attn)
        joined_projection = low_back(high_dot(normed_in, wq))
        query_raw = joined_projection[:, :query_columns].reshape(TOTAL_TOKENS, QUERY_HEADS, HEAD_DIM)
        key_unnormed = joined_projection[:, query_columns:query_columns + key_value_columns].reshape(TOTAL_TOKENS, KEY_VALUE_HEADS, HEAD_DIM)
        value_unnormed = joined_projection[:, query_columns + key_value_columns:].reshape(TOTAL_TOKENS, KEY_VALUE_HEADS, HEAD_DIM)
        query_n = query_raw * row_scale(query_raw) * gain_query
        key_n = key_unnormed * row_scale(key_unnormed) * gain_key
        query_b = low(rotate(query_n, cosine, sine_part) * HEAD_DIM ** (-0.5))
        key_batched = low(rotate(key_n, cosine, sine_part))
        value_batched = low(value_unnormed)
        query_s = query_b.reshape(PACKED_SEQUENCES, PACKED_LENGTH, QUERY_HEADS, HEAD_DIM).transpose(0, 2, 1, 3)
        key_sequences = key_batched.reshape(PACKED_SEQUENCES, PACKED_LENGTH, KEY_VALUE_HEADS, HEAD_DIM).transpose(0, 2, 1, 3)
        value_sequences = value_batched.reshape(PACKED_SEQUENCES, PACKED_LENGTH, KEY_VALUE_HEADS, HEAD_DIM).transpose(0, 2, 1, 3)
        segment_s = segments.reshape(PACKED_SEQUENCES, PACKED_LENGTH)
        heads_out = lax.map(jax.checkpoint(sequence_attention), (query_s, key_sequences, value_sequences, segment_s))
        attended = heads_out.transpose(0, 2, 1, 3).reshape(TOTAL_TOKENS, query_columns)
        attended = low_back(low(attended))
        branch_one = low_back(high_dot(attended, wo.T))
        middle = inputs + branch_one
        normed_mid = low(middle * row_scale(middle) * gain_ffn)
        gate_pre = low_back(high_dot(normed_mid, wg))
        up_pre = low_back(high_dot(normed_mid, wu))
        hidden = low(jax.nn.silu(gate_pre) * up_pre)
        branch_two = low_back(high_dot(hidden, wd.T))
        return middle + branch_two
    operands = (layer_input.astype(jnp.float32), query_key_value_weight.astype(jnp.float32), w_out.astype(jnp.float32), w_gate.astype(jnp.float32), w_up.astype(jnp.float32), w_down.astype(jnp.float32), g_attn, g_ffn, g_query, g_key)
    output, pull = jax.vjp(forward, *operands)
    grads = pull(cotangent.astype(jnp.float32))
    return (output.astype(jnp.bfloat16), grads[0].astype(jnp.bfloat16), grads[1], grads[2], grads[3], grads[4], grads[5], grads[6], grads[7], grads[8], grads[9])
```

```python
import functools

import jax
import jax.numpy as jnp
from jax import lax
from jax.experimental import pallas as pl
from jax.experimental.pallas import tpu as pltpu
from jax.sharding import Mesh
from jax.sharding import PartitionSpec as P

QUERY_HEADS = 20
KEY_VALUE_HEADS = 5
HEAD_DIM = 64
GROUP = QUERY_HEADS // KEY_VALUE_HEADS
QUERY_COLUMNS = QUERY_HEADS * HEAD_DIM
KEY_COLUMNS = KEY_VALUE_HEADS * HEAD_DIM
NORM_EPS = 1e-06

ALL = ("y", "core", "zh", "zl", "x")
SEQ = ("zh", "zl", "x")
TEAM = ("core", "zl", "x")
CHIPS = ("zl", "x")

bf16 = jnp.bfloat16
f32 = jnp.float32


def dot_nn(left, right):
    return jnp.dot(left, right, preferred_element_type=f32)


def dot_nt(left, right):
    return lax.dot_general(left, right, (((1,), (1,)), ((), ())), preferred_element_type=f32)


def dot_tn(left, right):
    return lax.dot_general(left, right, (((0,), (0,)), ((), ())), preferred_element_type=f32)


def row_scale(values):
    return lax.rsqrt(jnp.mean(values * values, axis=-1, keepdims=True) + NORM_EPS)


def head_norm(values):
    scale = lax.rsqrt(jnp.mean(values * values, axis=-1, keepdims=True) + NORM_EPS)
    return values * scale, scale


def turn(values):
    half = HEAD_DIM // 2
    return jnp.concatenate([-values[:, half:], values[:, :half]], axis=1)


def turn_back(values):
    half = HEAD_DIM // 2
    return jnp.concatenate([values[:, half:], -values[:, :half]], axis=1)


def heads_forward_kernel(qkv_ref, cos_ref, sin_ref, gq_ref, gk_ref, q_ref, kv_ref):
    cosine, sine = cos_ref[...], sin_ref[...]
    for head in range(QUERY_HEADS + KEY_VALUE_HEADS):
        columns = slice(head * HEAD_DIM, (head + 1) * HEAD_DIM)
        normed, _ = head_norm(qkv_ref[:, columns])
        if head < QUERY_HEADS:
            scaled = normed * gq_ref[...]
            turned = (scaled * cosine + turn(scaled) * sine) * (HEAD_DIM**-0.5)
            q_ref[:, columns] = turned.astype(bf16)
        else:
            scaled = normed * gk_ref[...]
            turned = scaled * cosine + turn(scaled) * sine
            place = slice((head - QUERY_HEADS) * HEAD_DIM, (head - QUERY_HEADS + 1) * HEAD_DIM)
            kv_ref[:, place] = turned.astype(bf16)
    kv_ref[:, KEY_COLUMNS:] = qkv_ref[:, QUERY_COLUMNS + KEY_COLUMNS :].astype(bf16)


def heads_backward_kernel(
    back, qkv_ref, cos_ref, sin_ref, gq_ref, gk_ref, dq_ref, own_ref, *refs
):
    received = refs[:back]
    grad_ref, gain_ref = refs[back:]
    cosine, sine = cos_ref[...], sin_ref[...]
    kv_grad = own_ref[...]
    for piece in received:
        kv_grad = kv_grad + piece[...].astype(f32)
    totals = [jnp.zeros((1, HEAD_DIM), f32), jnp.zeros((1, HEAD_DIM), f32)]
    for head in range(QUERY_HEADS + KEY_VALUE_HEADS):
        columns = slice(head * HEAD_DIM, (head + 1) * HEAD_DIM)
        normed, scale = head_norm(qkv_ref[:, columns])
        is_key = int(head >= QUERY_HEADS)
        if is_key:
            place = slice((head - QUERY_HEADS) * HEAD_DIM, (head - QUERY_HEADS + 1) * HEAD_DIM)
            grad = kv_grad[:, place]
            gain = gk_ref[...]
        else:
            grad = dq_ref[:, columns] * (HEAD_DIM**-0.5)
            gain = gq_ref[...]
        grad = grad * cosine + turn_back(grad * sine)
        totals[is_key] = totals[is_key] + jnp.sum(grad * normed, axis=0, keepdims=True)
        weighted = grad * gain
        inner = jnp.mean(weighted * normed, axis=-1, keepdims=True)
        grad_ref[:, columns] = (scale * (weighted - normed * inner)).astype(bf16)
    grad_ref[:, QUERY_COLUMNS + KEY_COLUMNS :] = kv_grad[:, KEY_COLUMNS:].astype(bf16)
    gain_ref[...] = jnp.concatenate(totals, axis=1)


def block_masks(back, tokens, pos_ref):
    key = lax.broadcasted_iota(jnp.int32, (tokens, GROUP * tokens), 0)
    query = lax.broadcasted_iota(jnp.int32, (tokens, GROUP * tokens), 1) % tokens
    offset = key - query
    low = -pos_ref[...]
    masks = [(offset <= 0) & (offset >= low)]
    for step in range(1, back + 1):
        masks.append(offset - step * tokens >= low)
    return masks


def stack_heads(ref, group):
    return jnp.concatenate(
        [
            ref[:, (group * GROUP + m) * HEAD_DIM : (group * GROUP + m + 1) * HEAD_DIM]
            for m in range(GROUP)
        ],
        axis=0,
    )


def key_value(ref, group):
    key = ref[:, group * HEAD_DIM : (group + 1) * HEAD_DIM]
    value = ref[:, KEY_COLUMNS + group * HEAD_DIM : KEY_COLUMNS + (group + 1) * HEAD_DIM]
    return key, value


def attend_forward_kernel(back, pos_ref, q_ref, *refs):
    kv_refs = refs[: back + 1]
    out_ref, inverse_ref = refs[back + 1 :]
    tokens = q_ref.shape[0]
    masks = block_masks(back, tokens, pos_ref)
    inverse_ref[...] = jnp.zeros_like(inverse_ref)
    for group in range(KEY_VALUE_HEADS):
        queries = stack_heads(q_ref, group)
        total = jnp.zeros((1, GROUP * tokens), f32)
        summed = jnp.zeros((HEAD_DIM, GROUP * tokens), f32)
        for step in range(back + 1):
            key, value = key_value(kv_refs[step], group)
            exponent = jnp.where(masks[step], jnp.exp(dot_nt(key, queries)), 0.0)
            total = total + jnp.sum(exponent, axis=0, keepdims=True)
            summed = summed + dot_tn(value, exponent.astype(bf16))
        inverse = 1.0 / total
        inverse_ref[group : group + 1, :] = inverse
        heads = summed * inverse
        for m in range(GROUP):
            head = group * GROUP + m
            out_ref[:, head * HEAD_DIM : (head + 1) * HEAD_DIM] = (
                heads[:, m * tokens : (m + 1) * tokens].T.astype(bf16)
            )


def attend_backward_kernel(back, pos_ref, q_ref, do_ref, inverse_ref, *refs):
    kv_refs = refs[: back + 1]
    dq_ref = refs[back + 1]
    dkv_refs = refs[back + 2 :]
    tokens = q_ref.shape[0]
    masks = block_masks(back, tokens, pos_ref)
    for group in range(KEY_VALUE_HEADS):
        queries = stack_heads(q_ref, group)
        out_grads = stack_heads(do_ref, group)
        inverse = inverse_ref[group : group + 1, :]
        chances, chance_grads = [], []
        row_dot = jnp.zeros((1, GROUP * tokens), f32)
        for step in range(back + 1):
            key, value = key_value(kv_refs[step], group)
            chance = jnp.where(masks[step], jnp.exp(dot_nt(key, queries)) * inverse, 0.0)
            chance_grad = dot_nt(value, out_grads)
            row_dot = row_dot + jnp.sum(chance * chance_grad, axis=0, keepdims=True)
            chances.append(chance)
            chance_grads.append(chance_grad)
        query_grad = jnp.zeros((HEAD_DIM, GROUP * tokens), f32)
        for step in range(back + 1):
            key, _ = key_value(kv_refs[step], group)
            score_grad = (chances[step] * (chance_grads[step] - row_dot)).astype(bf16)
            target = dkv_refs[step]
            target[:, group * HEAD_DIM : (group + 1) * HEAD_DIM] = dot_nn(
                score_grad, queries
            ).astype(target.dtype)
            target[:, KEY_COLUMNS + group * HEAD_DIM : KEY_COLUMNS + (group + 1) * HEAD_DIM] = (
                dot_nn(chances[step].astype(bf16), out_grads).astype(target.dtype)
            )
            query_grad = query_grad + dot_tn(key, score_grad)
        for m in range(GROUP):
            head = group * GROUP + m
            dq_ref[:, head * HEAD_DIM : (head + 1) * HEAD_DIM] = query_grad[
                :, m * tokens : (m + 1) * tokens
            ].T


def whole(kernel, out_shapes, name, flops, moved):
    return pl.pallas_call(
        kernel,
        out_shape=out_shapes,
        name=name,
        compiler_params=pltpu.CompilerParams(vmem_limit_bytes=48 << 20),
        cost_estimate=pl.CostEstimate(flops=flops, transcendentals=0, bytes_accessed=moved),
    )


def swap(value, axis, k):
    n = lax.axis_size(axis)
    return lax.ppermute(value, axis, [(i, i ^ k) for i in range(n)])


def shifted(value, step):
    n = lax.axis_size(SEQ)
    return lax.ppermute(value, SEQ, [(i, i + step) for i in range(n) if 0 <= i + step < n])


def spread_columns(pieces):
    team = lax.axis_size(TEAM)
    rows = pieces[0].shape[0]
    ny, nzh = lax.axis_size("y"), lax.axis_size("zh")
    blocks = jnp.concatenate([p.reshape(rows, team, -1) for p in pieces], axis=2)
    blocks = blocks.transpose(1, 0, 2)
    blocks = lax.all_to_all(blocks, TEAM, 0, 0, tiled=True)
    width = blocks.shape[2]
    nc = lax.axis_size("core")
    block = blocks.reshape(1, nc, 1, -1, width)
    full = jnp.zeros((ny, nc, nzh, block.shape[3], width), bf16)
    y, zh = lax.axis_index("y"), lax.axis_index("zh")
    far = [block] + [swap(block, "zh", b) for b in range(1, nzh)]
    for b in range(nzh):
        for a in range(ny):
            piece = far[b] if a == 0 else swap(far[b], "y", a)
            full = lax.dynamic_update_slice(full, piece, (y ^ a, 0, zh ^ b, 0, 0))
    return full.reshape(-1, width)


def reduce_rows(partial, shape):
    y, zh = lax.axis_index("y"), lax.axis_index("zh")
    ny, nzh = lax.axis_size("y"), lax.axis_size("zh")
    partial = partial.reshape(shape)
    total = lax.dynamic_index_in_dim(partial, y, 0, keepdims=False).astype(f32)
    for a in range(1, ny):
        total = total + swap(
            lax.dynamic_index_in_dim(partial, y ^ a, 0, keepdims=False), "y", a
        ).astype(f32)
    out = lax.dynamic_index_in_dim(total, zh, 1, keepdims=False)
    for b in range(1, nzh):
        out = out + swap(
            lax.dynamic_index_in_dim(total, zh ^ b, 1, keepdims=False).astype(bf16), "zh", b
        ).astype(f32)
    return out


def collect_columns(partial, count):
    ny, nzh, nc = lax.axis_size("y"), lax.axis_size("zh"), lax.axis_size("core")
    team = lax.axis_size(TEAM)
    total = reduce_rows(partial, (ny, nc, nzh, -1, partial.shape[1]))
    blocks = total.astype(bf16).reshape(team, -1, partial.shape[1])
    blocks = lax.all_to_all(blocks, TEAM, 0, 0, tiled=True)
    rows = blocks.shape[1]
    width = partial.shape[1] // count
    return [
        blocks[:, :, i * width : (i + 1) * width]
        .transpose(1, 0, 2)
        .reshape(rows, team * width)
        .astype(f32)
        for i in range(count)
    ]


def team_sum(partial):
    nc = lax.axis_size("core")
    chips = lax.axis_size(CHIPS)
    core = lax.axis_index("core")
    width = partial.shape[1]
    halves = partial.reshape(nc, -1, width)
    total = lax.dynamic_index_in_dim(halves, core, 0, keepdims=False).astype(f32)
    for k in range(1, nc):
        total = total + swap(
            lax.dynamic_index_in_dim(halves, core ^ k, 0, keepdims=False), "core", k
        ).astype(f32)
    blocks = total.astype(bf16).reshape(chips, -1, width)
    blocks = lax.all_to_all(blocks, CHIPS, 0, 0, tiled=True)
    return jnp.sum(blocks.astype(f32), axis=0)


def row_team(value):
    tokens = value.shape[0]
    ny, nc, nzh = lax.axis_size("y"), lax.axis_size("core"), lax.axis_size("zh")
    chips, team = lax.axis_size(CHIPS), lax.axis_size(TEAM)
    split = value.reshape(tokens, ny, nc, nzh, chips, -1).transpose(2, 4, 0, 1, 3, 5)
    split = split.reshape(team, tokens, -1)
    return lax.all_to_all(split, TEAM, 0, 0, tiled=True).reshape(team * tokens, -1)


def row_grads(row_side, column_side):
    ny, nzh = lax.axis_size("y"), lax.axis_size("zh")
    partial = dot_tn(row_side, column_side).astype(bf16)
    return reduce_rows(partial, (ny, 1, nzh, -1, partial.shape[1])).reshape(-1, partial.shape[1])


def sum_all(value):
    for axis in ("core", "x", "y", "zl", "zh"):
        k = 1
        while k < lax.axis_size(axis):
            value = value + swap(value, axis, k)
            k *= 2
    return value


def local(
    layer_input,
    segments,
    positions,
    query_key_value_weight,
    w_out,
    w_gate,
    w_up,
    w_down,
    g_attn,
    g_ffn,
    g_query,
    g_key,
    cotangent,
):
    tokens, model = layer_input.shape
    back = lax.axis_size(SEQ) // 2
    ff = w_gate.shape[1] // lax.axis_size(TEAM)

    inputs = layer_input.astype(f32)
    scale_in = row_scale(inputs)
    normed_in = inputs * scale_in
    normed_low = (normed_in * g_attn).astype(bf16)

    qkv_full = lax.all_gather(query_key_value_weight, ALL, axis=0, tiled=True)
    out_full = lax.all_gather(w_out, ALL, axis=0, tiled=True)
    gate_up = spread_columns([w_gate, w_up])
    down = spread_columns([w_down])
    grads_out = lax.all_gather(cotangent, TEAM, axis=0, tiled=True)

    joined = dot_nn(normed_low, qkv_full)

    half = HEAD_DIM // 2
    frequency = 10000.0 ** (-jnp.arange(half, dtype=f32) / half)
    angles = positions.astype(f32)[:, None] * frequency[None, :]
    angles = jnp.concatenate([angles, angles], axis=-1)
    cosine, sine = jnp.cos(angles), jnp.sin(angles)
    gq, gk = g_query[None, :], g_key[None, :]
    query_low, kv_low = whole(
        heads_forward_kernel,
        (
            jax.ShapeDtypeStruct((tokens, QUERY_COLUMNS), bf16),
            jax.ShapeDtypeStruct((tokens, 2 * KEY_COLUMNS), bf16),
        ),
        "heads_forward",
        tokens * 1920 * 20,
        tokens * 1920 * 6,
    )(joined, cosine, sine, gq, gk)

    kv_blocks = [kv_low] + [shifted(kv_low, step) for step in range(1, back + 1)]
    tiled_positions = jnp.tile(positions[None, :], (1, GROUP))
    attended, inverse = whole(
        functools.partial(attend_forward_kernel, back),
        (
            jax.ShapeDtypeStruct((tokens, QUERY_COLUMNS), bf16),
            jax.ShapeDtypeStruct((8, GROUP * tokens), f32),
        ),
        "attend_forward",
        4 * tokens * tokens * (back + 1) * QUERY_COLUMNS,
        tokens * 2000 * 10,
    )(tiled_positions, query_low, *kv_blocks)

    middle = inputs + dot_nt(attended, out_full)
    scale_mid = row_scale(middle)
    normed_mid = middle * scale_mid
    mid_low = (normed_mid * g_ffn).astype(bf16)
    mid_team = lax.all_gather(mid_low, TEAM, axis=0, tiled=True)

    gate_pre = dot_nn(mid_team, gate_up[:, :ff])
    up_pre = dot_nn(mid_team, gate_up[:, ff:])
    sigmoid_gate = jax.nn.sigmoid(gate_pre)
    activated = gate_pre * sigmoid_gate
    hidden = (activated * up_pre).astype(bf16)
    hidden_grad = dot_nn(grads_out, down)
    slope = sigmoid_gate * (1.0 + gate_pre * (1.0 - sigmoid_gate))
    gate_grad = (hidden_grad * up_pre * slope).astype(bf16)
    up_grad = (hidden_grad * activated).astype(bf16)
    gate_up_grad = jnp.concatenate([gate_grad, up_grad], axis=1)
    mid_grad = team_sum(dot_nt(gate_up_grad, gate_up).astype(bf16))
    branch_two = team_sum(dot_nt(hidden, down).astype(bf16))
    result = (middle + branch_two).astype(bf16)

    w_down_grad = collect_columns(dot_tn(grads_out, hidden).astype(bf16), 1)[0]
    w_gate_grad, w_up_grad = collect_columns(dot_tn(mid_team, gate_up_grad).astype(bf16), 2)

    weighted = mid_grad * g_ffn
    ffn_gain = jnp.sum(mid_grad * normed_mid, axis=0)
    middle_grad = cotangent.astype(f32) + scale_mid * (
        weighted - normed_mid * jnp.mean(weighted * normed_mid, axis=-1, keepdims=True)
    )
    branch_grad = middle_grad.astype(bf16)
    head_grads = dot_nn(branch_grad, out_full).astype(bf16)

    results = whole(
        functools.partial(attend_backward_kernel, back),
        (
            jax.ShapeDtypeStruct((tokens, QUERY_COLUMNS), f32),
            jax.ShapeDtypeStruct((tokens, 2 * KEY_COLUMNS), f32),
        )
        + (jax.ShapeDtypeStruct((tokens, 2 * KEY_COLUMNS), bf16),) * back,
        "attend_backward",
        10 * tokens * tokens * (back + 1) * QUERY_COLUMNS,
        tokens * 2000 * 20,
    )(tiled_positions, query_low, head_grads, inverse, *kv_blocks)
    query_grad, own_grad, far_grads = results[0], results[1], results[2:]
    received = [shifted(grad, -(i + 1)) for i, grad in enumerate(far_grads)]
    joined_grad, head_gains = whole(
        functools.partial(heads_backward_kernel, back),
        (
            jax.ShapeDtypeStruct((tokens, joined.shape[1]), bf16),
            jax.ShapeDtypeStruct((1, 2 * HEAD_DIM), f32),
        ),
        "heads_backward",
        tokens * 1920 * 30,
        tokens * 1920 * 16,
    )(joined, cosine, sine, gq, gk, query_grad, own_grad, *received)

    attended_team = lax.all_gather(attended, TEAM, axis=0, tiled=True)
    w_out_grad = row_grads(row_team(branch_grad), attended_team)
    joined_team = lax.all_gather(joined_grad, TEAM, axis=0, tiled=True)
    w_qkv_grad = row_grads(row_team(normed_low), joined_team)

    normed_in_grad = dot_nt(joined_grad, qkv_full)
    weighted_in = normed_in_grad * g_attn
    attn_gain = jnp.sum(normed_in_grad * normed_in, axis=0)
    input_grad = (
        middle_grad
        + scale_in
        * (weighted_in - normed_in * jnp.mean(weighted_in * normed_in, axis=-1, keepdims=True))
    ).astype(bf16)

    gains = sum_all(
        jnp.concatenate([attn_gain, ffn_gain, head_gains[0]], axis=0).reshape(-1, 128)
    ).reshape(-1)
    return (
        result,
        input_grad,
        w_qkv_grad,
        w_out_grad,
        w_gate_grad,
        w_up_grad,
        w_down_grad,
        gains[:model],
        gains[model : 2 * model],
        gains[2 * model : 2 * model + HEAD_DIM],
        gains[2 * model + HEAD_DIM :],
    )


def solution(mesh):
    inner, outer = mesh.devices.shape
    split = Mesh(mesh.devices.reshape(inner // 2, 2, 2, 2, outer // 4), ALL)
    rows, whole_array = P(ALL, None), P()
    in_specs = (rows, P(ALL), P(ALL)) + (rows,) * 5 + (whole_array,) * 4 + (rows,)
    out_specs = (rows,) * 7 + (whole_array,) * 4
    return jax.shard_map(local, mesh=split, in_specs=in_specs, out_specs=out_specs, check_vma=False)
```

```python
import functools

import jax
import jax.numpy as jnp
from jax import lax
from jax.experimental import pallas as pl
from jax.experimental.pallas import tpu as pltpu
from jax.sharding import Mesh
from jax.sharding import PartitionSpec as P

QUERY_HEADS = 20
KEY_VALUE_HEADS = 5
HEAD_DIM = 64
GROUP = QUERY_HEADS // KEY_VALUE_HEADS
QUERY_COLUMNS = QUERY_HEADS * HEAD_DIM
KEY_COLUMNS = KEY_VALUE_HEADS * HEAD_DIM
NORM_EPS = 1e-06

ALL = ("y", "core", "zh", "zl", "x")
SEQ = ("zh", "zl", "x")
TEAM = ("core", "zl", "x")
CHIPS = ("zl", "x")

bf16 = jnp.bfloat16
f32 = jnp.float32


def dot_nn(left, right):
    return jnp.dot(left, right, preferred_element_type=f32)


def dot_nt(left, right):
    return lax.dot_general(left, right, (((1,), (1,)), ((), ())), preferred_element_type=f32)


def dot_tn(left, right):
    return lax.dot_general(left, right, (((0,), (0,)), ((), ())), preferred_element_type=f32)


def row_scale(values):
    return lax.rsqrt(jnp.mean(values * values, axis=-1, keepdims=True) + NORM_EPS)


def head_norm(values):
    scale = lax.rsqrt(jnp.mean(values * values, axis=-1, keepdims=True) + NORM_EPS)
    return values * scale, scale


def turn(values):
    half = HEAD_DIM // 2
    return jnp.concatenate([-values[:, half:], values[:, :half]], axis=1)


def turn_back(values):
    half = HEAD_DIM // 2
    return jnp.concatenate([values[:, half:], -values[:, :half]], axis=1)


def block_head(ref, head):
    block, start = divmod(head * HEAD_DIM, ref.shape[2])
    return ref[block, :, start : start + HEAD_DIM].astype(f32)


def block_store(ref, head, value):
    block, start = divmod(head * HEAD_DIM, ref.shape[2])
    ref[block, :, start : start + HEAD_DIM] = value


def heads_forward_kernel(qkv_ref, cos_ref, sin_ref, gq_ref, gk_ref, q_ref, kv_ref):
    cosine, sine = cos_ref[...], sin_ref[...]
    for head in range(QUERY_HEADS + KEY_VALUE_HEADS):
        columns = slice(head * HEAD_DIM, (head + 1) * HEAD_DIM)
        normed, _ = head_norm(block_head(qkv_ref, head))
        if head < QUERY_HEADS:
            scaled = normed * gq_ref[...]
            turned = (scaled * cosine + turn(scaled) * sine) * (HEAD_DIM**-0.5)
            q_ref[:, columns] = turned.astype(bf16)
        else:
            scaled = normed * gk_ref[...]
            turned = scaled * cosine + turn(scaled) * sine
            place = slice((head - QUERY_HEADS) * HEAD_DIM, (head - QUERY_HEADS + 1) * HEAD_DIM)
            kv_ref[:, place] = turned.astype(bf16)
    for head in range(KEY_VALUE_HEADS):
        place = slice(KEY_COLUMNS + head * HEAD_DIM, KEY_COLUMNS + (head + 1) * HEAD_DIM)
        value = block_head(qkv_ref, QUERY_HEADS + KEY_VALUE_HEADS + head)
        kv_ref[:, place] = value.astype(bf16)


def heads_backward_kernel(
    back, qkv_ref, cos_ref, sin_ref, gq_ref, gk_ref, dq_ref, own_ref, *refs
):
    received = refs[:back]
    grad_ref, gain_ref = refs[back:]
    cosine, sine = cos_ref[...], sin_ref[...]
    kv_grad = own_ref[...]
    for piece in received:
        kv_grad = kv_grad + piece[...].astype(f32)
    totals = [jnp.zeros((1, HEAD_DIM), f32), jnp.zeros((1, HEAD_DIM), f32)]
    for head in range(QUERY_HEADS + KEY_VALUE_HEADS):
        columns = slice(head * HEAD_DIM, (head + 1) * HEAD_DIM)
        normed, scale = head_norm(block_head(qkv_ref, head))
        is_key = int(head >= QUERY_HEADS)
        if is_key:
            place = slice((head - QUERY_HEADS) * HEAD_DIM, (head - QUERY_HEADS + 1) * HEAD_DIM)
            grad = kv_grad[:, place]
            gain = gk_ref[...]
        else:
            grad = dq_ref[:, columns] * (HEAD_DIM**-0.5)
            gain = gq_ref[...]
        grad = grad * cosine + turn_back(grad * sine)
        totals[is_key] = totals[is_key] + jnp.sum(grad * normed, axis=0, keepdims=True)
        weighted = grad * gain
        inner = jnp.mean(weighted * normed, axis=-1, keepdims=True)
        block_store(grad_ref, head, (scale * (weighted - normed * inner)).astype(bf16))
    for head in range(KEY_VALUE_HEADS):
        place = slice(KEY_COLUMNS + head * HEAD_DIM, KEY_COLUMNS + (head + 1) * HEAD_DIM)
        block_store(grad_ref, QUERY_HEADS + KEY_VALUE_HEADS + head, kv_grad[:, place].astype(bf16))
    count, tokens, width = grad_ref.shape
    for head in range(QUERY_HEADS + 2 * KEY_VALUE_HEADS, count * width // HEAD_DIM):
        block_store(grad_ref, head, jnp.zeros((tokens, HEAD_DIM), bf16))
    gain_ref[...] = jnp.concatenate(totals, axis=1)


def block_masks(back, tokens, pos_ref):
    key = lax.broadcasted_iota(jnp.int32, (tokens, GROUP * tokens), 0)
    query = lax.broadcasted_iota(jnp.int32, (tokens, GROUP * tokens), 1) % tokens
    offset = key - query
    low = -pos_ref[...]
    masks = [(offset <= 0) & (offset >= low)]
    for step in range(1, back + 1):
        masks.append(offset - step * tokens >= low)
    return masks


def stack_heads(ref, group):
    return jnp.concatenate(
        [
            ref[:, (group * GROUP + m) * HEAD_DIM : (group * GROUP + m + 1) * HEAD_DIM]
            for m in range(GROUP)
        ],
        axis=0,
    )


def key_value(ref, group):
    key = ref[:, group * HEAD_DIM : (group + 1) * HEAD_DIM]
    value = ref[:, KEY_COLUMNS + group * HEAD_DIM : KEY_COLUMNS + (group + 1) * HEAD_DIM]
    return key, value


def attend_forward_kernel(back, pos_ref, q_ref, *refs):
    kv_refs = refs[: back + 1]
    out_ref, inverse_ref = refs[back + 1 :]
    tokens = q_ref.shape[0]
    masks = block_masks(back, tokens, pos_ref)
    inverse_ref[...] = jnp.zeros_like(inverse_ref)
    for group in range(KEY_VALUE_HEADS):
        queries = stack_heads(q_ref, group)
        total = jnp.zeros((1, GROUP * tokens), f32)
        summed = jnp.zeros((HEAD_DIM, GROUP * tokens), f32)
        for step in range(back + 1):
            key, value = key_value(kv_refs[step], group)
            exponent = jnp.where(masks[step], jnp.exp(dot_nt(key, queries)), 0.0)
            total = total + jnp.sum(exponent, axis=0, keepdims=True)
            summed = summed + dot_tn(value, exponent.astype(bf16))
        inverse = 1.0 / total
        inverse_ref[group : group + 1, :] = inverse
        heads = summed * inverse
        for m in range(GROUP):
            head = group * GROUP + m
            out_ref[:, head * HEAD_DIM : (head + 1) * HEAD_DIM] = (
                heads[:, m * tokens : (m + 1) * tokens].T.astype(bf16)
            )


def attend_backward_kernel(back, pos_ref, q_ref, do_ref, inverse_ref, *refs):
    kv_refs = refs[: back + 1]
    dq_ref = refs[back + 1]
    dkv_refs = refs[back + 2 :]
    tokens = q_ref.shape[0]
    masks = block_masks(back, tokens, pos_ref)
    for group in range(KEY_VALUE_HEADS):
        queries = stack_heads(q_ref, group)
        out_grads = stack_heads(do_ref, group)
        inverse = inverse_ref[group : group + 1, :]
        chances, chance_grads = [], []
        row_dot = jnp.zeros((1, GROUP * tokens), f32)
        for step in range(back + 1):
            key, value = key_value(kv_refs[step], group)
            chance = jnp.where(masks[step], jnp.exp(dot_nt(key, queries)) * inverse, 0.0)
            chance_grad = dot_nt(value, out_grads)
            row_dot = row_dot + jnp.sum(chance * chance_grad, axis=0, keepdims=True)
            chances.append(chance)
            chance_grads.append(chance_grad)
        query_grad = jnp.zeros((HEAD_DIM, GROUP * tokens), f32)
        for step in range(back + 1):
            key, _ = key_value(kv_refs[step], group)
            score_grad = (chances[step] * (chance_grads[step] - row_dot)).astype(bf16)
            target = dkv_refs[step]
            target[:, group * HEAD_DIM : (group + 1) * HEAD_DIM] = dot_nn(
                score_grad, queries
            ).astype(target.dtype)
            target[:, KEY_COLUMNS + group * HEAD_DIM : KEY_COLUMNS + (group + 1) * HEAD_DIM] = (
                dot_nn(chances[step].astype(bf16), out_grads).astype(target.dtype)
            )
            query_grad = query_grad + dot_tn(key, score_grad)
        for m in range(GROUP):
            head = group * GROUP + m
            dq_ref[:, head * HEAD_DIM : (head + 1) * HEAD_DIM] = query_grad[
                :, m * tokens : (m + 1) * tokens
            ].T


def ffn_dz_kernel(count, offsets, grads_ref, *refs):
    blocks, out_ref = refs[:-1], refs[-1]
    total = jnp.zeros(out_ref.shape, f32)
    for i, column, piece in pieces_of(blocks, offsets, count):
        total = total + dot_nn(grads_ref[:, column], piece[...])
    out_ref[...] = total


def ffn_mid_kernel(count, offsets, mid_ref, dz_ref, *refs):
    blocks = len(refs) // 2 - 2
    gates, ups = refs[:blocks], refs[blocks : 2 * blocks]
    hidden_ref, gate_grad_ref, up_grad_ref, out_ref = refs[2 * blocks :]
    gate = jnp.zeros(dz_ref.shape, f32)
    up = jnp.zeros(dz_ref.shape, f32)
    for i, column, piece in pieces_of(gates, offsets, count):
        gate = gate + dot_nn(mid_ref[:, column], piece[...])
    for i, column, piece in pieces_of(ups, offsets, count):
        up = up + dot_nn(mid_ref[:, column], piece[...])
    sigmoid = 1.0 / (1.0 + jnp.exp(-gate))
    activated = gate * sigmoid
    hidden_ref[...] = (activated * up).astype(bf16)
    hidden_grad = dz_ref[...]
    slope = sigmoid * (1.0 + gate * (1.0 - sigmoid))
    gate_grad = (hidden_grad * up * slope).astype(bf16)
    up_grad = (hidden_grad * activated).astype(bf16)
    gate_grad_ref[...] = gate_grad
    up_grad_ref[...] = up_grad
    up_pieces = list(pieces_of(ups, offsets, count))
    for i, column, piece in pieces_of(gates, offsets, count):
        out_ref[:, column] = (
            dot_nt(gate_grad, piece[...]) + dot_nt(up_grad, up_pieces[i][2][...])
        ).astype(bf16)


def ffn_out_kernel(count, offsets, hidden_ref, *refs):
    blocks, out_ref = refs[:-1], refs[-1]
    for i, column, piece in pieces_of(blocks, offsets, count):
        out_ref[:, column] = dot_nt(hidden_ref[...], piece[...]).astype(bf16)


def weight_grad_kernel(rows_ref, columns_ref, out_ref):
    out_ref[...] = dot_tn(rows_ref[...], columns_ref[...]).astype(bf16)


def weight_grad(row_side, column_side, name):
    tokens, model = row_side.shape
    width = column_side.shape[1]
    ny, nc, nzh = lax.axis_size("y"), lax.axis_size("core"), lax.axis_size("zh")
    rows = model // (ny * nc * nzh)

    def put(r):
        y, rest = r // (nc * nzh), r % (nc * nzh)
        return ((y * nzh + rest % nzh) * nc + rest // nzh, 0)

    return pl.pallas_call(
        weight_grad_kernel,
        out_shape=jax.ShapeDtypeStruct((model, width), bf16),
        grid=(model // rows,),
        in_specs=[
            pl.BlockSpec((tokens, rows), lambda r: (0, r)),
            pl.BlockSpec((tokens, width), lambda r: (0, 0)),
        ],
        out_specs=pl.BlockSpec((rows, width), put),
        name=name,
        compiler_params=pltpu.CompilerParams(vmem_limit_bytes=32 << 20),
        cost_estimate=pl.CostEstimate(
            flops=2 * tokens * model * width,
            transcendentals=0,
            bytes_accessed=2 * (tokens * model + tokens * width + model * width),
        ),
    )(row_side, column_side)


def pieces_of(blocks, offsets, count):
    i = 0
    for block in blocks:
        rows = block.shape[0] // count
        for c in range(count):
            column = pl.ds(pl.multiple_of(offsets[i], 128), rows)
            yield i, column, block.at[c * rows : (c + 1) * rows, :]
            i += 1


def by_tokens(kernel, offsets, token_arrays, blocks, outs, name, flops):
    tokens = token_arrays[0].shape[0]
    chunk = min(256, tokens)
    blocks = [block.reshape(-1, block.shape[-1]) for block in blocks]
    moved = 2 * sum(b.size for b in blocks) + 2 * sum(t.size for t in token_arrays)
    row = lambda width: pl.BlockSpec((chunk, width), lambda t, o: (t, 0))
    return pl.pallas_call(
        functools.partial(kernel, lax.axis_size("core")),
        out_shape=tuple(jax.ShapeDtypeStruct((tokens, width), kind) for width, kind in outs),
        grid_spec=pltpu.PrefetchScalarGridSpec(
            num_scalar_prefetch=1,
            grid=(tokens // chunk,),
            in_specs=[row(t.shape[1]) for t in token_arrays]
            + [pl.BlockSpec(b.shape, lambda t, o: (0, 0)) for b in blocks],
            out_specs=tuple(row(width) for width, _ in outs),
        ),
        name=name,
        compiler_params=pltpu.CompilerParams(vmem_limit_bytes=48 << 20),
        cost_estimate=pl.CostEstimate(flops=flops, transcendentals=0, bytes_accessed=moved),
    )(offsets, *token_arrays, *blocks)


def whole(kernel, out_shapes, name, flops, moved):
    return pl.pallas_call(
        kernel,
        out_shape=out_shapes,
        name=name,
        compiler_params=pltpu.CompilerParams(vmem_limit_bytes=48 << 20),
        cost_estimate=pl.CostEstimate(flops=flops, transcendentals=0, bytes_accessed=moved),
    )


def swap(value, axis, k):
    n = lax.axis_size(axis)
    return lax.ppermute(value, axis, [(i, i ^ k) for i in range(n)])


def shifted(value, step):
    n = lax.axis_size(SEQ)
    return lax.ppermute(value, SEQ, [(i, i + step) for i in range(n) if 0 <= i + step < n])


def tie(*values):
    return lax.optimization_barrier(values)


def team_columns(pieces):
    team, nc = lax.axis_size(TEAM), lax.axis_size("core")
    rows = pieces[0].shape[0]
    blocks = jnp.concatenate([p.reshape(rows, team, -1) for p in pieces], axis=2)
    blocks = lax.all_to_all(blocks.transpose(1, 0, 2), TEAM, 0, 0, tiled=True)
    return blocks.reshape(1, nc, 1, -1, blocks.shape[2])


def exchange(block, axis):
    return [block] + [swap(block, axis, k) for k in range(1, lax.axis_size(axis))]


def place(pieces):
    y, zh = lax.axis_index("y"), lax.axis_index("zh")
    _, nc, _, rest, width = pieces[0][0].shape
    full = jnp.zeros((lax.axis_size("y"), nc, lax.axis_size("zh"), rest, width), bf16)
    for b, row in enumerate(pieces):
        for a, piece in enumerate(row):
            full = lax.dynamic_update_slice(full, piece, (y ^ a, 0, zh ^ b, 0, 0))
    return full.reshape(-1, width)


def reduce_y(partial):
    y = lax.axis_index("y")
    total = lax.dynamic_index_in_dim(partial, y, 0, keepdims=False).astype(f32)
    for a in range(1, lax.axis_size("y")):
        total = total + swap(
            lax.dynamic_index_in_dim(partial, y ^ a, 0, keepdims=False), "y", a
        ).astype(f32)
    return total


def reduce_zh(total):
    zh = lax.axis_index("zh")
    out = lax.dynamic_index_in_dim(total, zh, 1, keepdims=False)
    for b in range(1, lax.axis_size("zh")):
        out = out + swap(
            lax.dynamic_index_in_dim(total, zh ^ b, 1, keepdims=False).astype(bf16), "zh", b
        ).astype(f32)
    return out


def return_columns(totals):
    team = lax.axis_size(TEAM)
    parts = [total.astype(bf16).reshape(team, -1, total.shape[-1]) for total in totals]
    blocks = lax.all_to_all(jnp.concatenate(parts, axis=2), TEAM, 0, 0, tiled=True)
    grads, start = [], 0
    for part in parts:
        width = part.shape[2]
        grad = blocks[:, :, start : start + width].transpose(1, 0, 2)
        grads.append(grad.reshape(grad.shape[0], -1).astype(f32))
        start += width
    return grads


def team_core(partial):
    nc = lax.axis_size("core")
    core = lax.axis_index("core")
    halves = partial.reshape(nc, -1, partial.shape[1])
    total = lax.dynamic_index_in_dim(halves, core, 0, keepdims=False).astype(f32)
    for k in range(1, nc):
        total = total + swap(
            lax.dynamic_index_in_dim(halves, core ^ k, 0, keepdims=False), "core", k
        ).astype(f32)
    return total.astype(bf16)


def team_chips(total):
    chips, chip = lax.axis_size(CHIPS), lax.axis_index(CHIPS)
    blocks = total.reshape(chips, -1, total.shape[1])
    block = lambda i: lax.dynamic_index_in_dim(blocks, i, 0, keepdims=False)
    far = [
        lax.ppermute(block(chip ^ k), CHIPS, [(i, i ^ k) for i in range(chips)])
        for k in range(1, chips)
    ]
    out = block(chip).astype(f32)
    for piece in far:
        out = out + piece.astype(f32)
    return out


def team_sum(partial):
    return team_chips(team_core(partial))


def row_team(value):
    tokens = value.shape[0]
    ny, nc, nzh = lax.axis_size("y"), lax.axis_size("core"), lax.axis_size("zh")
    chips, team = lax.axis_size(CHIPS), lax.axis_size(TEAM)
    split = value.reshape(tokens, ny, nc, nzh, chips, -1).transpose(2, 4, 0, 1, 3, 5)
    split = split.reshape(team, tokens, -1)
    return lax.all_to_all(split, TEAM, 0, 0, tiled=True).reshape(team * tokens, -1)


def own_rows(value):
    ny, nc, nzh = lax.axis_size("y"), lax.axis_size("core"), lax.axis_size("zh")
    split = value.reshape(value.shape[0], ny, nc, nzh, lax.axis_size(CHIPS), -1)
    split = lax.dynamic_index_in_dim(split, lax.axis_index("core"), 2, keepdims=False)
    split = lax.dynamic_index_in_dim(split, lax.axis_index(CHIPS), 3, keepdims=False)
    return split.reshape(value.shape[0], -1)


def sum_over(value, axes):
    for axis in axes:
        k = 1
        while k < lax.axis_size(axis):
            value = value + swap(value, axis, k)
            k *= 2
    return value


def local(
    layer_input,
    segments,
    positions,
    query_key_value_weight,
    w_out,
    w_gate,
    w_up,
    w_down,
    g_attn,
    g_ffn,
    g_query,
    g_key,
    cotangent,
):
    tokens, model = layer_input.shape
    back = lax.axis_size(SEQ) // 2
    ff = w_gate.shape[1] // lax.axis_size(TEAM)

    inputs = layer_input.astype(f32)
    scale_in = row_scale(inputs)
    normed_in = inputs * scale_in
    normed_low = (normed_in * g_attn).astype(bf16)

    team = lax.axis_size(TEAM)
    joined_columns = query_key_value_weight.shape[1]
    padded = -(-joined_columns // (128 * team)) * 128 * team

    y, zh = lax.axis_index("y"), lax.axis_index("zh")
    ny, nc, nzh = lax.axis_size("y"), lax.axis_size("core"), lax.axis_size("zh")
    width = model // (ny * nc * nzh)
    offsets = jnp.stack(
        [
            (((y ^ a) * nc + c) * nzh + (zh ^ b)) * width
            for b in range(nzh)
            for a in range(ny)
            for c in range(nc)
        ]
    ).astype(jnp.int32)

    normed_team = lax.all_gather(normed_low, TEAM, axis=0, tiled=True)
    qkv_block = team_columns([jnp.pad(query_key_value_weight, ((0, 0), (0, padded - joined_columns)))])
    qkv_block, w_down, w_out = tie(qkv_block, w_down, w_out)
    qkv_near, qkv_far = exchange(qkv_block, "y"), exchange(qkv_block, "zh")
    out_near = exchange(w_out[None, None], "zh")
    down_block = team_columns([w_down])
    out_part = [exchange(piece, "y") for piece in out_near]
    qkv_part = place([qkv_near] + [exchange(piece, "y") for piece in qkv_far[1:]])
    out_rows = jnp.zeros((ny, nzh) + w_out.shape, bf16)
    for b, row in enumerate(out_part):
        for a, piece in enumerate(row):
            out_rows = lax.dynamic_update_slice(out_rows, piece, (y ^ a, zh ^ b, 0, 0))

    normed_team, qkv_part, out_rows, down_block, w_gate = tie(
        normed_team, qkv_part, out_rows, down_block, w_gate
    )
    out_full = lax.all_gather(out_rows, TEAM, axis=0, tiled=False)
    out_full = (
        out_full.reshape((nc, lax.axis_size(CHIPS)) + out_rows.shape)
        .transpose(2, 0, 3, 1, 4, 5)
        .reshape(model, -1)
    )
    down_far, down_near = exchange(down_block, "zh"), exchange(down_block, "y")
    joined_team = dot_nn(normed_team, qkv_part).astype(bf16)
    joined = lax.all_to_all(
        joined_team.reshape(team, tokens, -1), TEAM, 0, 0, tiled=True
    )
    joined, down_near = tie(joined, down_near)

    half = HEAD_DIM // 2
    frequency = 10000.0 ** (-jnp.arange(half, dtype=f32) / half)
    angles = positions.astype(f32)[:, None] * frequency[None, :]
    angles = jnp.concatenate([angles, angles], axis=-1)
    cosine, sine = jnp.cos(angles), jnp.sin(angles)
    gq, gk = g_query[None, :], g_key[None, :]
    query_low, kv_low = whole(
        heads_forward_kernel,
        (
            jax.ShapeDtypeStruct((tokens, QUERY_COLUMNS), bf16),
            jax.ShapeDtypeStruct((tokens, 2 * KEY_COLUMNS), bf16),
        ),
        "heads_forward",
        tokens * 1920 * 20,
        tokens * 1920 * 6,
    )(joined, cosine, sine, gq, gk)

    kv_blocks = [kv_low] + [shifted(kv_low, step) for step in range(1, back + 1)]
    kv_blocks, down_far, w_gate, cotangent_in = tie(kv_blocks, down_far, w_gate, cotangent)
    gate_block = team_columns([w_gate])
    down_blocks = down_near + sum([exchange(piece, "y") for piece in down_far[1:]], [])
    grads_out = lax.all_gather(cotangent_in, TEAM, axis=0, tiled=True)
    tiled_positions = jnp.tile(positions[None, :], (1, GROUP))
    attended, inverse = whole(
        functools.partial(attend_forward_kernel, back),
        (
            jax.ShapeDtypeStruct((tokens, QUERY_COLUMNS), bf16),
            jax.ShapeDtypeStruct((8, GROUP * tokens), f32),
        ),
        "attend_forward",
        4 * tokens * tokens * (back + 1) * QUERY_COLUMNS,
        tokens * 2000 * 10,
    )(tiled_positions, query_low, *kv_blocks)

    attended, out_full, gate_block, w_up = tie(attended, out_full, gate_block, w_up)
    gate_far, gate_near = exchange(gate_block, "zh"), exchange(gate_block, "y")
    up_block = team_columns([w_up])
    middle = inputs + dot_nt(attended, out_full)
    scale_mid = row_scale(middle)
    normed_mid = middle * scale_mid
    mid_low = (normed_mid * g_ffn).astype(bf16)
    mid_team = lax.all_gather(mid_low, TEAM, axis=0, tiled=True)

    products = 2 * mid_team.shape[0] * model * ff
    grads_out, down_blocks, gate_far, gate_near, up_block = tie(
        grads_out, down_blocks, gate_far, gate_near, up_block
    )
    up_far, up_near = exchange(up_block, "zh"), exchange(up_block, "y")
    gate_blocks = gate_near + sum([exchange(piece, "y") for piece in gate_far[1:]], [])
    (hidden_grad,) = by_tokens(
        ffn_dz_kernel, offsets, [grads_out], down_blocks, [(ff, f32)], "ffn_dz", products
    )
    mid_team, hidden_grad, gate_blocks, up_far, up_near, attended_in = tie(
        mid_team, hidden_grad, gate_blocks, up_far, up_near, attended
    )
    up_blocks = up_near + sum([exchange(piece, "y") for piece in up_far[1:]], [])
    attended_team = lax.all_gather(attended_in, TEAM, axis=0, tiled=True)
    hidden, gate_grad, up_grad, mid_part = by_tokens(
        ffn_mid_kernel,
        offsets,
        [mid_team, hidden_grad],
        gate_blocks + up_blocks,
        [(ff, bf16), (ff, bf16), (ff, bf16), (model, bf16)],
        "ffn_mid",
        4 * products,
    )

    scatter = lambda part: lax.psum_scatter(part, ("y", "zh"), scatter_dimension=0, tiled=True)
    mid_part, attended_team, hidden = tie(mid_part, attended_team, hidden)
    mid_half = team_core(mid_part)
    down_part = weight_grad(grads_out, hidden, "down_grad")
    down_sum = scatter(down_part)
    mid_half, hidden, _ = tie(mid_half, hidden, down_part)
    mid_grad = team_chips(mid_half)
    branch_half = team_core(
        by_tokens(
            ffn_out_kernel, offsets, [hidden], down_blocks, [(model, bf16)], "ffn_out", products
        )[0]
    )
    mid_grad, branch_half, mid_team, gate_grad, up_grad = tie(
        mid_grad, branch_half, mid_team, gate_grad, up_grad
    )

    weighted = mid_grad * g_ffn
    ffn_gain = jnp.sum(mid_grad * normed_mid, axis=0)
    middle_grad = cotangent.astype(f32) + scale_mid * (
        weighted - normed_mid * jnp.mean(weighted * normed_mid, axis=-1, keepdims=True)
    )
    branch_grad = middle_grad.astype(bf16)
    head_grads = dot_nn(branch_grad, out_full).astype(bf16)
    results = whole(
        functools.partial(attend_backward_kernel, back),
        (
            jax.ShapeDtypeStruct((tokens, QUERY_COLUMNS), f32),
            jax.ShapeDtypeStruct((tokens, 2 * KEY_COLUMNS), f32),
        )
        + (jax.ShapeDtypeStruct((tokens, 2 * KEY_COLUMNS), bf16),) * back,
        "attend_backward",
        10 * tokens * tokens * (back + 1) * QUERY_COLUMNS,
        tokens * 2000 * 20,
    )(tiled_positions, query_low, head_grads, inverse, *kv_blocks)
    query_grad, own_grad, far_grads = results[0], results[1], results[2:]
    far_grads, gate_grad, mid_team_in = tie(far_grads, gate_grad, mid_team)
    gate_part = weight_grad(mid_team_in, gate_grad, "gate_grad")
    received = [shifted(grad, -(i + 1)) for i, grad in enumerate(far_grads)]
    received, down_sum, gate_part, up_grad = tie(received, down_sum, gate_part, up_grad)
    gate_sum = scatter(gate_part)
    joined_grad, head_gains = whole(
        functools.partial(heads_backward_kernel, back),
        (
            jax.ShapeDtypeStruct(joined.shape, bf16),
            jax.ShapeDtypeStruct((1, 2 * HEAD_DIM), f32),
        ),
        "heads_backward",
        tokens * 1920 * 30,
        tokens * 1920 * 16,
    )(joined, cosine, sine, gq, gk, query_grad, own_grad, *received)

    joined_grad, up_grad, mid_team = tie(joined_grad, up_grad, mid_team)
    up_part = weight_grad(mid_team, up_grad, "up_grad")
    joined_grad = lax.all_to_all(joined_grad, TEAM, 0, 0, tiled=True).reshape(-1, padded // team)
    joined_grad, up_part, down_sum = tie(joined_grad, up_part, down_sum)
    up_sum = scatter(up_part)
    normed_in_grad = team_sum(dot_nt(joined_grad, qkv_part).astype(bf16))
    normed_in_grad, gate_sum, joined_grad, down_sum, branch_grad, branch_half = tie(
        normed_in_grad, gate_sum, joined_grad, down_sum, branch_grad, branch_half
    )
    qkv_sum = reduce_zh(
        reduce_y(
            dot_tn(normed_team, joined_grad).astype(bf16).reshape(ny, nc, nzh, -1, padded // team)
        )
    )
    w_down_grad, w_gate_grad = return_columns([down_sum, gate_sum])
    out_part = dot_tn(row_team(branch_grad), attended_team).astype(bf16)
    out_sum = reduce_y(out_part.reshape(ny, 1, nzh, -1, out_part.shape[1]))
    branch_two = team_chips(branch_half)
    weighted_in = normed_in_grad * g_attn
    attn_gain = jnp.sum(normed_in_grad * normed_in, axis=0)
    input_grad = (
        middle_grad
        + scale_in
        * (weighted_in - normed_in * jnp.mean(weighted_in * normed_in, axis=-1, keepdims=True))
    ).astype(bf16)

    gains = sum_over(
        jnp.concatenate([attn_gain, ffn_gain, head_gains[0]], axis=0).reshape(-1, 128),
        ("core", "x", "y"),
    )
    gains, up_sum, qkv_sum, out_sum, branch_two = tie(
        gains, up_sum, qkv_sum, out_sum, branch_two
    )
    w_up_grad, w_qkv_grad = return_columns([up_sum, qkv_sum])
    w_qkv_grad = w_qkv_grad[:, :joined_columns]
    gains = sum_over(gains, ("zl", "zh")).reshape(-1)
    w_out_grad = reduce_zh(out_sum).reshape(-1, out_sum.shape[-1])
    result = (middle + branch_two).astype(bf16)
    return (
        result,
        input_grad,
        w_qkv_grad,
        w_out_grad,
        w_gate_grad,
        w_up_grad,
        w_down_grad,
        gains[:model],
        gains[model : 2 * model],
        gains[2 * model : 2 * model + HEAD_DIM],
        gains[2 * model + HEAD_DIM :],
    )


def solution(mesh):
    inner, outer = mesh.devices.shape
    split = Mesh(mesh.devices.reshape(inner // 2, 2, 2, 2, outer // 4), ALL)
    rows, whole_array = P(ALL, None), P()
    in_specs = (rows, P(ALL), P(ALL)) + (rows,) * 5 + (whole_array,) * 4 + (rows,)
    out_specs = (rows,) * 7 + (whole_array,) * 4
    return jax.shard_map(local, mesh=split, in_specs=in_specs, out_specs=out_specs, check_vma=False)
```

```python
import functools

import jax
import jax.numpy as jnp
from jax import lax
from jax.experimental import pallas as pl
from jax.experimental.pallas import tpu as pltpu
from jax.sharding import Mesh
from jax.sharding import PartitionSpec as P

QUERY_HEADS = 20
KEY_VALUE_HEADS = 5
HEAD_DIM = 64
GROUP = QUERY_HEADS // KEY_VALUE_HEADS
QUERY_COLUMNS = QUERY_HEADS * HEAD_DIM
KEY_COLUMNS = KEY_VALUE_HEADS * HEAD_DIM
NORM_EPS = 1e-06

ALL = ("y", "core", "zh", "zl", "x")
SEQ = ("zh", "zl", "x")
TEAM = ("core", "zl", "x")
CHIPS = ("zl", "x")

bf16 = jnp.bfloat16
f32 = jnp.float32


def dot_nn(left, right):
    return jnp.dot(left, right, preferred_element_type=f32)


def dot_nt(left, right):
    return lax.dot_general(left, right, (((1,), (1,)), ((), ())), preferred_element_type=f32)


def dot_tn(left, right):
    return lax.dot_general(left, right, (((0,), (0,)), ((), ())), preferred_element_type=f32)


def row_scale(values):
    return lax.rsqrt(jnp.mean(values * values, axis=-1, keepdims=True) + NORM_EPS)


def head_norm(values):
    scale = lax.rsqrt(jnp.mean(values * values, axis=-1, keepdims=True) + NORM_EPS)
    return values * scale, scale


def turn(values):
    half = HEAD_DIM // 2
    return jnp.concatenate([-values[:, half:], values[:, :half]], axis=1)


def turn_back(values):
    half = HEAD_DIM // 2
    return jnp.concatenate([values[:, half:], -values[:, :half]], axis=1)


def block_head(ref, head):
    block, start = divmod(head * HEAD_DIM, ref.shape[2])
    return ref[block, :, start : start + HEAD_DIM].astype(f32)


def block_store(ref, head, value):
    block, start = divmod(head * HEAD_DIM, ref.shape[2])
    ref[block, :, start : start + HEAD_DIM] = value


def heads_forward_kernel(qkv_ref, cos_ref, sin_ref, gq_ref, gk_ref, q_ref, kv_ref):
    cosine, sine = cos_ref[...], sin_ref[...]
    for head in range(QUERY_HEADS + KEY_VALUE_HEADS):
        columns = slice(head * HEAD_DIM, (head + 1) * HEAD_DIM)
        normed, _ = head_norm(block_head(qkv_ref, head))
        if head < QUERY_HEADS:
            scaled = normed * gq_ref[...]
            turned = (scaled * cosine + turn(scaled) * sine) * (HEAD_DIM**-0.5)
            q_ref[:, columns] = turned.astype(bf16)
        else:
            scaled = normed * gk_ref[...]
            turned = scaled * cosine + turn(scaled) * sine
            place = slice((head - QUERY_HEADS) * HEAD_DIM, (head - QUERY_HEADS + 1) * HEAD_DIM)
            kv_ref[:, place] = turned.astype(bf16)
    for head in range(KEY_VALUE_HEADS):
        place = slice(KEY_COLUMNS + head * HEAD_DIM, KEY_COLUMNS + (head + 1) * HEAD_DIM)
        value = block_head(qkv_ref, QUERY_HEADS + KEY_VALUE_HEADS + head)
        kv_ref[:, place] = value.astype(bf16)


def heads_backward_kernel(
    back, qkv_ref, cos_ref, sin_ref, gq_ref, gk_ref, dq_ref, own_ref, *refs
):
    received = refs[:back]
    grad_ref, gain_ref = refs[back:]
    cosine, sine = cos_ref[...], sin_ref[...]
    kv_grad = own_ref[...]
    for piece in received:
        kv_grad = kv_grad + piece[...].astype(f32)
    totals = [jnp.zeros((1, HEAD_DIM), f32), jnp.zeros((1, HEAD_DIM), f32)]
    for head in range(QUERY_HEADS + KEY_VALUE_HEADS):
        columns = slice(head * HEAD_DIM, (head + 1) * HEAD_DIM)
        normed, scale = head_norm(block_head(qkv_ref, head))
        is_key = int(head >= QUERY_HEADS)
        if is_key:
            place = slice((head - QUERY_HEADS) * HEAD_DIM, (head - QUERY_HEADS + 1) * HEAD_DIM)
            grad = kv_grad[:, place]
            gain = gk_ref[...]
        else:
            grad = dq_ref[:, columns] * (HEAD_DIM**-0.5)
            gain = gq_ref[...]
        grad = grad * cosine + turn_back(grad * sine)
        totals[is_key] = totals[is_key] + jnp.sum(grad * normed, axis=0, keepdims=True)
        weighted = grad * gain
        inner = jnp.mean(weighted * normed, axis=-1, keepdims=True)
        block_store(grad_ref, head, (scale * (weighted - normed * inner)).astype(bf16))
    for head in range(KEY_VALUE_HEADS):
        place = slice(KEY_COLUMNS + head * HEAD_DIM, KEY_COLUMNS + (head + 1) * HEAD_DIM)
        block_store(grad_ref, QUERY_HEADS + KEY_VALUE_HEADS + head, kv_grad[:, place].astype(bf16))
    count, tokens, width = grad_ref.shape
    for head in range(QUERY_HEADS + 2 * KEY_VALUE_HEADS, count * width // HEAD_DIM):
        block_store(grad_ref, head, jnp.zeros((tokens, HEAD_DIM), bf16))
    gain_ref[...] = jnp.concatenate(totals, axis=1)


def block_masks(back, tokens, pos_ref):
    key = lax.broadcasted_iota(jnp.int32, (tokens, GROUP * tokens), 0)
    query = lax.broadcasted_iota(jnp.int32, (tokens, GROUP * tokens), 1) % tokens
    offset = key - query
    low = -pos_ref[...]
    masks = [(offset <= 0) & (offset >= low)]
    for step in range(1, back + 1):
        masks.append(offset - step * tokens >= low)
    return masks


def stack_heads(ref, group):
    return jnp.concatenate(
        [
            ref[:, (group * GROUP + m) * HEAD_DIM : (group * GROUP + m + 1) * HEAD_DIM]
            for m in range(GROUP)
        ],
        axis=0,
    )


def key_value(ref, group):
    key = ref[:, group * HEAD_DIM : (group + 1) * HEAD_DIM]
    value = ref[:, KEY_COLUMNS + group * HEAD_DIM : KEY_COLUMNS + (group + 1) * HEAD_DIM]
    return key, value


def attend_forward_kernel(back, pos_ref, q_ref, *refs):
    kv_refs = refs[: back + 1]
    out_ref, inverse_ref = refs[back + 1 :]
    tokens = q_ref.shape[0]
    masks = block_masks(back, tokens, pos_ref)
    inverse_ref[...] = jnp.zeros_like(inverse_ref)
    for group in range(KEY_VALUE_HEADS):
        queries = stack_heads(q_ref, group)
        total = jnp.zeros((1, GROUP * tokens), f32)
        summed = jnp.zeros((HEAD_DIM, GROUP * tokens), f32)
        for step in range(back + 1):
            key, value = key_value(kv_refs[step], group)
            exponent = jnp.where(masks[step], jnp.exp(dot_nt(key, queries)), 0.0)
            total = total + jnp.sum(exponent, axis=0, keepdims=True)
            summed = summed + dot_tn(value, exponent.astype(bf16))
        inverse = 1.0 / total
        inverse_ref[group : group + 1, :] = inverse
        heads = summed * inverse
        for m in range(GROUP):
            head = group * GROUP + m
            out_ref[:, head * HEAD_DIM : (head + 1) * HEAD_DIM] = (
                heads[:, m * tokens : (m + 1) * tokens].T.astype(bf16)
            )


def attend_backward_kernel(back, pos_ref, q_ref, do_ref, inverse_ref, *refs):
    kv_refs = refs[: back + 1]
    dq_ref = refs[back + 1]
    dkv_refs = refs[back + 2 :]
    tokens = q_ref.shape[0]
    masks = block_masks(back, tokens, pos_ref)
    for group in range(KEY_VALUE_HEADS):
        queries = stack_heads(q_ref, group)
        out_grads = stack_heads(do_ref, group)
        inverse = inverse_ref[group : group + 1, :]
        chances, chance_grads = [], []
        row_dot = jnp.zeros((1, GROUP * tokens), f32)
        for step in range(back + 1):
            key, value = key_value(kv_refs[step], group)
            chance = jnp.where(masks[step], jnp.exp(dot_nt(key, queries)) * inverse, 0.0)
            chance_grad = dot_nt(value, out_grads)
            row_dot = row_dot + jnp.sum(chance * chance_grad, axis=0, keepdims=True)
            chances.append(chance)
            chance_grads.append(chance_grad)
        query_grad = jnp.zeros((HEAD_DIM, GROUP * tokens), f32)
        for step in range(back + 1):
            key, _ = key_value(kv_refs[step], group)
            score_grad = (chances[step] * (chance_grads[step] - row_dot)).astype(bf16)
            target = dkv_refs[step]
            target[:, group * HEAD_DIM : (group + 1) * HEAD_DIM] = dot_nn(
                score_grad, queries
            ).astype(target.dtype)
            target[:, KEY_COLUMNS + group * HEAD_DIM : KEY_COLUMNS + (group + 1) * HEAD_DIM] = (
                dot_nn(chances[step].astype(bf16), out_grads).astype(target.dtype)
            )
            query_grad = query_grad + dot_tn(key, score_grad)
        for m in range(GROUP):
            head = group * GROUP + m
            dq_ref[:, head * HEAD_DIM : (head + 1) * HEAD_DIM] = query_grad[
                :, m * tokens : (m + 1) * tokens
            ].T


def ffn_dz_kernel(count, offsets, grads_ref, *refs):
    blocks, out_ref = refs[:-1], refs[-1]
    total = jnp.zeros(out_ref.shape, f32)
    for i, column, piece in pieces_of(blocks, offsets, count):
        total = total + dot_nn(grads_ref[:, column], piece[...])
    out_ref[...] = total


def ffn_mid_kernel(count, offsets, mid_ref, dz_ref, *refs):
    blocks = len(refs) // 2 - 2
    gates, ups = refs[:blocks], refs[blocks : 2 * blocks]
    hidden_ref, gate_grad_ref, up_grad_ref, out_ref = refs[2 * blocks :]
    gate = jnp.zeros(dz_ref.shape, f32)
    up = jnp.zeros(dz_ref.shape, f32)
    for i, column, piece in pieces_of(gates, offsets, count):
        gate = gate + dot_nn(mid_ref[:, column], piece[...])
    for i, column, piece in pieces_of(ups, offsets, count):
        up = up + dot_nn(mid_ref[:, column], piece[...])
    sigmoid = 1.0 / (1.0 + jnp.exp(-gate))
    activated = gate * sigmoid
    hidden_ref[...] = (activated * up).astype(bf16)
    hidden_grad = dz_ref[...]
    slope = sigmoid * (1.0 + gate * (1.0 - sigmoid))
    gate_grad = (hidden_grad * up * slope).astype(bf16)
    up_grad = (hidden_grad * activated).astype(bf16)
    gate_grad_ref[...] = gate_grad
    up_grad_ref[...] = up_grad
    up_pieces = list(pieces_of(ups, offsets, count))
    for i, column, piece in pieces_of(gates, offsets, count):
        out_ref[:, column] = (
            dot_nt(gate_grad, piece[...]) + dot_nt(up_grad, up_pieces[i][2][...])
        ).astype(bf16)


def ffn_out_kernel(count, offsets, hidden_ref, *refs):
    blocks, out_ref = refs[:-1], refs[-1]
    for i, column, piece in pieces_of(blocks, offsets, count):
        out_ref[:, column] = dot_nt(hidden_ref[...], piece[...]).astype(bf16)


def weight_grad_kernel(rows_ref, columns_ref, out_ref):
    out_ref[...] = dot_tn(rows_ref[...], columns_ref[...]).astype(bf16)


def weight_grad(row_side, column_side, name):
    tokens, model = row_side.shape
    width = column_side.shape[1]
    ny, nc, nzh = lax.axis_size("y"), lax.axis_size("core"), lax.axis_size("zh")
    rows = model // (ny * nc * nzh)

    def put(r):
        y, rest = r // (nc * nzh), r % (nc * nzh)
        return ((y * nzh + rest % nzh) * nc + rest // nzh, 0)

    return pl.pallas_call(
        weight_grad_kernel,
        out_shape=jax.ShapeDtypeStruct((model, width), bf16),
        grid=(model // rows,),
        in_specs=[
            pl.BlockSpec((tokens, rows), lambda r: (0, r)),
            pl.BlockSpec((tokens, width), lambda r: (0, 0)),
        ],
        out_specs=pl.BlockSpec((rows, width), put),
        name=name,
        compiler_params=pltpu.CompilerParams(vmem_limit_bytes=32 << 20),
        cost_estimate=pl.CostEstimate(
            flops=2 * tokens * model * width,
            transcendentals=0,
            bytes_accessed=2 * (tokens * model + tokens * width + model * width),
        ),
    )(row_side, column_side)


def pieces_of(blocks, offsets, count):
    i = 0
    for block in blocks:
        rows = block.shape[0] // count
        for c in range(count):
            column = pl.ds(pl.multiple_of(offsets[i], 128), rows)
            yield i, column, block.at[c * rows : (c + 1) * rows, :]
            i += 1


def by_tokens(kernel, offsets, token_arrays, blocks, outs, name, flops):
    tokens = token_arrays[0].shape[0]
    chunk = min(256, tokens)
    blocks = [block.reshape(-1, block.shape[-1]) for block in blocks]
    moved = 2 * sum(b.size for b in blocks) + 2 * sum(t.size for t in token_arrays)
    row = lambda width: pl.BlockSpec((chunk, width), lambda t, o: (t, 0))
    return pl.pallas_call(
        functools.partial(kernel, lax.axis_size("core")),
        out_shape=tuple(jax.ShapeDtypeStruct((tokens, width), kind) for width, kind in outs),
        grid_spec=pltpu.PrefetchScalarGridSpec(
            num_scalar_prefetch=1,
            grid=(tokens // chunk,),
            in_specs=[row(t.shape[1]) for t in token_arrays]
            + [pl.BlockSpec(b.shape, lambda t, o: (0, 0)) for b in blocks],
            out_specs=tuple(row(width) for width, _ in outs),
        ),
        name=name,
        compiler_params=pltpu.CompilerParams(vmem_limit_bytes=48 << 20),
        cost_estimate=pl.CostEstimate(flops=flops, transcendentals=0, bytes_accessed=moved),
    )(offsets, *token_arrays, *blocks)


def whole(kernel, out_shapes, name, flops, moved):
    return pl.pallas_call(
        kernel,
        out_shape=out_shapes,
        name=name,
        compiler_params=pltpu.CompilerParams(vmem_limit_bytes=48 << 20),
        cost_estimate=pl.CostEstimate(flops=flops, transcendentals=0, bytes_accessed=moved),
    )


def swap(value, axis, k):
    n = lax.axis_size(axis)
    return lax.ppermute(value, axis, [(i, i ^ k) for i in range(n)])


def shifted(value, step):
    n = lax.axis_size(SEQ)
    return lax.ppermute(value, SEQ, [(i, i + step) for i in range(n) if 0 <= i + step < n])


def tie(*values):
    return lax.optimization_barrier(values)


def team_columns(pieces):
    team, nc = lax.axis_size(TEAM), lax.axis_size("core")
    rows = pieces[0].shape[0]
    blocks = jnp.concatenate([p.reshape(rows, team, -1) for p in pieces], axis=2)
    blocks = lax.all_to_all(blocks.transpose(1, 0, 2), TEAM, 0, 0, tiled=True)
    return blocks.reshape(1, nc, 1, -1, blocks.shape[2])


def exchange(block, axis):
    return [block] + [swap(block, axis, k) for k in range(1, lax.axis_size(axis))]


def place(pieces):
    y, zh = lax.axis_index("y"), lax.axis_index("zh")
    _, nc, _, rest, width = pieces[0][0].shape
    full = jnp.zeros((lax.axis_size("y"), nc, lax.axis_size("zh"), rest, width), bf16)
    for b, row in enumerate(pieces):
        for a, piece in enumerate(row):
            full = lax.dynamic_update_slice(full, piece, (y ^ a, 0, zh ^ b, 0, 0))
    return full.reshape(-1, width)


def reduce_y(partial):
    y = lax.axis_index("y")
    total = lax.dynamic_index_in_dim(partial, y, 0, keepdims=False).astype(f32)
    for a in range(1, lax.axis_size("y")):
        total = total + swap(
            lax.dynamic_index_in_dim(partial, y ^ a, 0, keepdims=False), "y", a
        ).astype(f32)
    return total


def reduce_zh(total):
    zh = lax.axis_index("zh")
    out = lax.dynamic_index_in_dim(total, zh, 1, keepdims=False)
    for b in range(1, lax.axis_size("zh")):
        out = out + swap(
            lax.dynamic_index_in_dim(total, zh ^ b, 1, keepdims=False).astype(bf16), "zh", b
        ).astype(f32)
    return out


def return_columns(totals):
    team = lax.axis_size(TEAM)
    parts = [total.astype(bf16).reshape(team, -1, total.shape[-1]) for total in totals]
    blocks = lax.all_to_all(jnp.concatenate(parts, axis=2), TEAM, 0, 0, tiled=True)
    grads, start = [], 0
    for part in parts:
        width = part.shape[2]
        grad = blocks[:, :, start : start + width].transpose(1, 0, 2)
        grads.append(grad.reshape(grad.shape[0], -1).astype(f32))
        start += width
    return grads


def team_core(partial):
    nc = lax.axis_size("core")
    core = lax.axis_index("core")
    halves = partial.reshape(nc, -1, partial.shape[1])
    total = lax.dynamic_index_in_dim(halves, core, 0, keepdims=False).astype(f32)
    for k in range(1, nc):
        total = total + swap(
            lax.dynamic_index_in_dim(halves, core ^ k, 0, keepdims=False), "core", k
        ).astype(f32)
    return total.astype(bf16)


def team_chips(total):
    chips, chip = lax.axis_size(CHIPS), lax.axis_index(CHIPS)
    blocks = total.reshape(chips, -1, total.shape[1])
    block = lambda i: lax.dynamic_index_in_dim(blocks, i, 0, keepdims=False)
    far = [
        lax.ppermute(block(chip ^ k), CHIPS, [(i, i ^ k) for i in range(chips)])
        for k in range(1, chips)
    ]
    out = block(chip).astype(f32)
    for piece in far:
        out = out + piece.astype(f32)
    return out


def team_sum(partial):
    return team_chips(team_core(partial))


def row_team(value):
    tokens = value.shape[0]
    ny, nc, nzh = lax.axis_size("y"), lax.axis_size("core"), lax.axis_size("zh")
    chips, team = lax.axis_size(CHIPS), lax.axis_size(TEAM)
    split = value.reshape(tokens, ny, nc, nzh, chips, -1).transpose(2, 4, 0, 1, 3, 5)
    split = split.reshape(team, tokens, -1)
    return lax.all_to_all(split, TEAM, 0, 0, tiled=True).reshape(team * tokens, -1)


def own_rows(value):
    ny, nc, nzh = lax.axis_size("y"), lax.axis_size("core"), lax.axis_size("zh")
    split = value.reshape(value.shape[0], ny, nc, nzh, lax.axis_size(CHIPS), -1)
    split = lax.dynamic_index_in_dim(split, lax.axis_index("core"), 2, keepdims=False)
    split = lax.dynamic_index_in_dim(split, lax.axis_index(CHIPS), 3, keepdims=False)
    return split.reshape(value.shape[0], -1)


def sum_over(value, axes):
    for axis in axes:
        k = 1
        while k < lax.axis_size(axis):
            value = value + swap(value, axis, k)
            k *= 2
    return value


def local(
    layer_input,
    segments,
    positions,
    query_key_value_weight,
    w_out,
    w_gate,
    w_up,
    w_down,
    g_attn,
    g_ffn,
    g_query,
    g_key,
    cotangent,
):
    tokens, model = layer_input.shape
    back = lax.axis_size(SEQ) // 2
    ff = w_gate.shape[1] // lax.axis_size(TEAM)

    inputs = layer_input.astype(f32)
    scale_in = row_scale(inputs)
    normed_in = inputs * scale_in
    normed_low = (normed_in * g_attn).astype(bf16)

    team = lax.axis_size(TEAM)
    joined_columns = query_key_value_weight.shape[1]
    padded = -(-joined_columns // (128 * team)) * 128 * team

    y, zh = lax.axis_index("y"), lax.axis_index("zh")
    ny, nc, nzh = lax.axis_size("y"), lax.axis_size("core"), lax.axis_size("zh")
    width = model // (ny * nc * nzh)
    offsets = jnp.stack(
        [
            (((y ^ a) * nc + c) * nzh + (zh ^ b)) * width
            for b in range(nzh)
            for a in range(ny)
            for c in range(nc)
        ]
    ).astype(jnp.int32)

    normed_team = lax.all_gather(normed_low, TEAM, axis=0, tiled=True)
    qkv_block = team_columns([jnp.pad(query_key_value_weight, ((0, 0), (0, padded - joined_columns)))])
    qkv_block, w_down, w_out = tie(qkv_block, w_down, w_out)
    qkv_near, qkv_far = exchange(qkv_block, "y"), exchange(qkv_block, "zh")
    out_near = exchange(w_out[None, None], "zh")
    down_block = team_columns([w_down])
    out_part = [exchange(piece, "y") for piece in out_near]
    qkv_part = place([qkv_near] + [exchange(piece, "y") for piece in qkv_far[1:]])
    out_rows = jnp.zeros((ny, nzh) + w_out.shape, bf16)
    for b, row in enumerate(out_part):
        for a, piece in enumerate(row):
            out_rows = lax.dynamic_update_slice(out_rows, piece, (y ^ a, zh ^ b, 0, 0))

    normed_team, qkv_part, out_rows, down_block, w_gate = tie(
        normed_team, qkv_part, out_rows, down_block, w_gate
    )
    out_full = lax.all_gather(out_rows, TEAM, axis=0, tiled=False)
    out_full = (
        out_full.reshape((nc, lax.axis_size(CHIPS)) + out_rows.shape)
        .transpose(2, 0, 3, 1, 4, 5)
        .reshape(model, -1)
    )
    down_far, down_near = exchange(down_block, "zh"), exchange(down_block, "y")
    joined_team = dot_nn(normed_team, qkv_part).astype(bf16)
    joined = lax.all_to_all(
        joined_team.reshape(team, tokens, -1), TEAM, 0, 0, tiled=True
    )
    joined, down_near = tie(joined, down_near)

    half = HEAD_DIM // 2
    frequency = 10000.0 ** (-jnp.arange(half, dtype=f32) / half)
    angles = positions.astype(f32)[:, None] * frequency[None, :]
    angles = jnp.concatenate([angles, angles], axis=-1)
    cosine, sine = jnp.cos(angles), jnp.sin(angles)
    gq, gk = g_query[None, :], g_key[None, :]
    query_low, kv_low = whole(
        heads_forward_kernel,
        (
            jax.ShapeDtypeStruct((tokens, QUERY_COLUMNS), bf16),
            jax.ShapeDtypeStruct((tokens, 2 * KEY_COLUMNS), bf16),
        ),
        "heads_forward",
        tokens * 1920 * 20,
        tokens * 1920 * 6,
    )(joined, cosine, sine, gq, gk)

    kv_blocks = [kv_low] + [shifted(kv_low, step) for step in range(1, back + 1)]
    kv_blocks, down_far, w_gate, cotangent_in = tie(kv_blocks, down_far, w_gate, cotangent)
    gate_block = team_columns([w_gate])
    down_blocks = down_near + sum([exchange(piece, "y") for piece in down_far[1:]], [])
    grads_out = lax.all_gather(cotangent_in, TEAM, axis=0, tiled=True)
    tiled_positions = jnp.tile(positions[None, :], (1, GROUP))
    attended, inverse = whole(
        functools.partial(attend_forward_kernel, back),
        (
            jax.ShapeDtypeStruct((tokens, QUERY_COLUMNS), bf16),
            jax.ShapeDtypeStruct((8, GROUP * tokens), f32),
        ),
        "attend_forward",
        4 * tokens * tokens * (back + 1) * QUERY_COLUMNS,
        tokens * 2000 * 10,
    )(tiled_positions, query_low, *kv_blocks)

    attended, out_full, gate_block, w_up = tie(attended, out_full, gate_block, w_up)
    gate_far, gate_near = exchange(gate_block, "zh"), exchange(gate_block, "y")
    up_block = team_columns([w_up])
    middle = inputs + dot_nt(attended, out_full)
    scale_mid = row_scale(middle)
    normed_mid = middle * scale_mid
    mid_low = (normed_mid * g_ffn).astype(bf16)
    mid_team = lax.all_gather(mid_low, TEAM, axis=0, tiled=True)

    products = 2 * mid_team.shape[0] * model * ff
    grads_out, down_blocks, gate_far, gate_near, up_block = tie(
        grads_out, down_blocks, gate_far, gate_near, up_block
    )
    up_far, up_near = exchange(up_block, "zh"), exchange(up_block, "y")
    gate_blocks = gate_near + sum([exchange(piece, "y") for piece in gate_far[1:]], [])
    (hidden_grad,) = by_tokens(
        ffn_dz_kernel, offsets, [grads_out], down_blocks, [(ff, f32)], "ffn_dz", products
    )
    mid_team, hidden_grad, gate_blocks, up_far, up_near, attended_in = tie(
        mid_team, hidden_grad, gate_blocks, up_far, up_near, attended
    )
    up_blocks = up_near + sum([exchange(piece, "y") for piece in up_far[1:]], [])
    attended_team = lax.all_gather(attended_in, TEAM, axis=0, tiled=True)
    hidden, gate_grad, up_grad, mid_part = by_tokens(
        ffn_mid_kernel,
        offsets,
        [mid_team, hidden_grad],
        gate_blocks + up_blocks,
        [(ff, bf16), (ff, bf16), (ff, bf16), (model, bf16)],
        "ffn_mid",
        4 * products,
    )

    scatter = lambda part: lax.psum_scatter(part, ("y", "zh"), scatter_dimension=0, tiled=True)
    mid_part, attended_team, hidden = tie(mid_part, attended_team, hidden)
    mid_half = team_core(mid_part)
    down_part = weight_grad(grads_out, hidden, "down_grad")
    down_sum = scatter(down_part)
    mid_half, hidden, _ = tie(mid_half, hidden, down_part)
    mid_grad = team_chips(mid_half)
    branch_half = team_core(
        by_tokens(
            ffn_out_kernel, offsets, [hidden], down_blocks, [(model, bf16)], "ffn_out", products
        )[0]
    )
    mid_grad, branch_half, mid_team, gate_grad, up_grad = tie(
        mid_grad, branch_half, mid_team, gate_grad, up_grad
    )

    weighted = mid_grad * g_ffn
    ffn_gain = jnp.sum(mid_grad * normed_mid, axis=0)
    middle_grad = cotangent.astype(f32) + scale_mid * (
        weighted - normed_mid * jnp.mean(weighted * normed_mid, axis=-1, keepdims=True)
    )
    branch_grad = middle_grad.astype(bf16)
    head_grads = dot_nn(branch_grad, out_full).astype(bf16)
    results = whole(
        functools.partial(attend_backward_kernel, back),
        (
            jax.ShapeDtypeStruct((tokens, QUERY_COLUMNS), f32),
            jax.ShapeDtypeStruct((tokens, 2 * KEY_COLUMNS), f32),
        )
        + (jax.ShapeDtypeStruct((tokens, 2 * KEY_COLUMNS), bf16),) * back,
        "attend_backward",
        10 * tokens * tokens * (back + 1) * QUERY_COLUMNS,
        tokens * 2000 * 20,
    )(tiled_positions, query_low, head_grads, inverse, *kv_blocks)
    query_grad, own_grad, far_grads = results[0], results[1], results[2:]
    far_grads, gate_grad, mid_team_in = tie(far_grads, gate_grad, mid_team)
    gate_part = weight_grad(mid_team_in, gate_grad, "gate_grad")
    received = [shifted(grad, -(i + 1)) for i, grad in enumerate(far_grads)]
    received, down_sum, gate_part, up_grad = tie(received, down_sum, gate_part, up_grad)
    gate_sum = scatter(gate_part)
    joined_grad, head_gains = whole(
        functools.partial(heads_backward_kernel, back),
        (
            jax.ShapeDtypeStruct(joined.shape, bf16),
            jax.ShapeDtypeStruct((1, 2 * HEAD_DIM), f32),
        ),
        "heads_backward",
        tokens * 1920 * 30,
        tokens * 1920 * 16,
    )(joined, cosine, sine, gq, gk, query_grad, own_grad, *received)

    joined_grad, up_grad, mid_team = tie(joined_grad, up_grad, mid_team)
    up_part = weight_grad(mid_team, up_grad, "up_grad")
    joined_grad = lax.all_to_all(joined_grad, TEAM, 0, 0, tiled=True).reshape(-1, padded // team)
    joined_grad, up_part, down_sum = tie(joined_grad, up_part, down_sum)
    up_sum = scatter(up_part)
    normed_half = team_core(dot_nt(joined_grad, qkv_part).astype(bf16))
    normed_half, branch_grad = tie(normed_half, branch_grad)
    normed_in_grad = team_chips(normed_half)
    branch_rows = row_team(branch_grad)
    normed_in_grad, gate_sum, joined_grad, down_sum, branch_rows, branch_half = tie(
        normed_in_grad, gate_sum, joined_grad, down_sum, branch_rows, branch_half
    )
    qkv_sum = reduce_zh(
        reduce_y(
            dot_tn(normed_team, joined_grad).astype(bf16).reshape(ny, nc, nzh, -1, padded // team)
        )
    )
    w_down_grad, w_gate_grad = return_columns([down_sum, gate_sum])
    out_part = dot_tn(branch_rows, attended_team).astype(bf16)
    out_sum = reduce_y(out_part.reshape(ny, 1, nzh, -1, out_part.shape[1]))
    branch_two = team_chips(branch_half)
    weighted_in = normed_in_grad * g_attn
    attn_gain = jnp.sum(normed_in_grad * normed_in, axis=0)
    input_grad = (
        middle_grad
        + scale_in
        * (weighted_in - normed_in * jnp.mean(weighted_in * normed_in, axis=-1, keepdims=True))
    ).astype(bf16)

    gains = sum_over(
        jnp.concatenate([attn_gain, ffn_gain, head_gains[0]], axis=0).reshape(-1, 128),
        ("core", "x"),
    )
    gains, up_sum, qkv_sum, out_sum, branch_two = tie(
        gains, up_sum, qkv_sum, out_sum, branch_two
    )
    w_up_grad, w_qkv_grad = return_columns([up_sum, qkv_sum])
    w_qkv_grad = w_qkv_grad[:, :joined_columns]
    gains = sum_over(gains, ("y", "zl", "zh")).reshape(-1)
    w_out_grad = reduce_zh(out_sum).reshape(-1, out_sum.shape[-1])
    result = (middle + branch_two).astype(bf16)
    return (
        result,
        input_grad,
        w_qkv_grad,
        w_out_grad,
        w_gate_grad,
        w_up_grad,
        w_down_grad,
        gains[:model],
        gains[model : 2 * model],
        gains[2 * model : 2 * model + HEAD_DIM],
        gains[2 * model + HEAD_DIM :],
    )


def solution(mesh):
    inner, outer = mesh.devices.shape
    split = Mesh(mesh.devices.reshape(inner // 2, 2, 2, 2, outer // 4), ALL)
    rows, whole_array = P(ALL, None), P()
    in_specs = (rows, P(ALL), P(ALL)) + (rows,) * 5 + (whole_array,) * 4 + (rows,)
    out_specs = (rows,) * 7 + (whole_array,) * 4
    return jax.shard_map(local, mesh=split, in_specs=in_specs, out_specs=out_specs, check_vma=False)
```

```python
import functools

import jax
import jax.numpy as jnp
from jax import lax
from jax.experimental import pallas as pl
from jax.experimental.pallas import tpu as pltpu
from jax.sharding import Mesh
from jax.sharding import PartitionSpec as P

QUERY_HEADS = 20
KEY_VALUE_HEADS = 5
HEAD_DIM = 64
GROUP = QUERY_HEADS // KEY_VALUE_HEADS
QUERY_COLUMNS = QUERY_HEADS * HEAD_DIM
KEY_COLUMNS = KEY_VALUE_HEADS * HEAD_DIM
NORM_EPS = 1e-06

ALL = ("y", "core", "zh", "zl", "x")
SEQ = ("zh", "zl", "x")
TEAM = ("core", "zl", "x")
CHIPS = ("zl", "x")

bf16 = jnp.bfloat16
f32 = jnp.float32


def dot_nn(left, right):
    return jnp.dot(left, right, preferred_element_type=f32)


def dot_nt(left, right):
    return lax.dot_general(left, right, (((1,), (1,)), ((), ())), preferred_element_type=f32)


def dot_tn(left, right):
    return lax.dot_general(left, right, (((0,), (0,)), ((), ())), preferred_element_type=f32)


def row_scale(values):
    return lax.rsqrt(jnp.mean(values * values, axis=-1, keepdims=True) + NORM_EPS)


def head_norm(values):
    scale = lax.rsqrt(jnp.mean(values * values, axis=-1, keepdims=True) + NORM_EPS)
    return values * scale, scale


def turn(values):
    half = HEAD_DIM // 2
    return jnp.concatenate([-values[:, half:], values[:, :half]], axis=1)


def turn_back(values):
    half = HEAD_DIM // 2
    return jnp.concatenate([values[:, half:], -values[:, :half]], axis=1)


def block_head(ref, head):
    block, start = divmod(head * HEAD_DIM, ref.shape[2])
    return ref[block, :, start : start + HEAD_DIM].astype(f32)


def block_store(ref, head, value):
    block, start = divmod(head * HEAD_DIM, ref.shape[2])
    ref[block, :, start : start + HEAD_DIM] = value


def heads_forward_kernel(qkv_ref, cos_ref, sin_ref, gq_ref, gk_ref, q_ref, kv_ref):
    cosine, sine = cos_ref[...], sin_ref[...]
    for head in range(QUERY_HEADS + KEY_VALUE_HEADS):
        columns = slice(head * HEAD_DIM, (head + 1) * HEAD_DIM)
        normed, _ = head_norm(block_head(qkv_ref, head))
        if head < QUERY_HEADS:
            scaled = normed * gq_ref[...]
            turned = (scaled * cosine + turn(scaled) * sine) * (HEAD_DIM**-0.5)
            q_ref[:, columns] = turned.astype(bf16)
        else:
            scaled = normed * gk_ref[...]
            turned = scaled * cosine + turn(scaled) * sine
            place = slice((head - QUERY_HEADS) * HEAD_DIM, (head - QUERY_HEADS + 1) * HEAD_DIM)
            kv_ref[:, place] = turned.astype(bf16)
    for head in range(KEY_VALUE_HEADS):
        place = slice(KEY_COLUMNS + head * HEAD_DIM, KEY_COLUMNS + (head + 1) * HEAD_DIM)
        value = block_head(qkv_ref, QUERY_HEADS + KEY_VALUE_HEADS + head)
        kv_ref[:, place] = value.astype(bf16)


def heads_backward_kernel(
    back, qkv_ref, cos_ref, sin_ref, gq_ref, gk_ref, dq_ref, own_ref, *refs
):
    received = refs[:back]
    grad_ref, gain_ref = refs[back:]
    cosine, sine = cos_ref[...], sin_ref[...]
    kv_grad = own_ref[...]
    for piece in received:
        kv_grad = kv_grad + piece[...].astype(f32)
    totals = [jnp.zeros((1, HEAD_DIM), f32), jnp.zeros((1, HEAD_DIM), f32)]
    for head in range(QUERY_HEADS + KEY_VALUE_HEADS):
        columns = slice(head * HEAD_DIM, (head + 1) * HEAD_DIM)
        normed, scale = head_norm(block_head(qkv_ref, head))
        is_key = int(head >= QUERY_HEADS)
        if is_key:
            place = slice((head - QUERY_HEADS) * HEAD_DIM, (head - QUERY_HEADS + 1) * HEAD_DIM)
            grad = kv_grad[:, place]
            gain = gk_ref[...]
        else:
            grad = dq_ref[:, columns] * (HEAD_DIM**-0.5)
            gain = gq_ref[...]
        grad = grad * cosine + turn_back(grad * sine)
        totals[is_key] = totals[is_key] + jnp.sum(grad * normed, axis=0, keepdims=True)
        weighted = grad * gain
        inner = jnp.mean(weighted * normed, axis=-1, keepdims=True)
        block_store(grad_ref, head, (scale * (weighted - normed * inner)).astype(bf16))
    for head in range(KEY_VALUE_HEADS):
        place = slice(KEY_COLUMNS + head * HEAD_DIM, KEY_COLUMNS + (head + 1) * HEAD_DIM)
        block_store(grad_ref, QUERY_HEADS + KEY_VALUE_HEADS + head, kv_grad[:, place].astype(bf16))
    count, tokens, width = grad_ref.shape
    for head in range(QUERY_HEADS + 2 * KEY_VALUE_HEADS, count * width // HEAD_DIM):
        block_store(grad_ref, head, jnp.zeros((tokens, HEAD_DIM), bf16))
    gain_ref[...] = jnp.concatenate(totals, axis=1)


def block_masks(back, tokens, pos_ref):
    key = lax.broadcasted_iota(jnp.int32, (tokens, GROUP * tokens), 0)
    query = lax.broadcasted_iota(jnp.int32, (tokens, GROUP * tokens), 1) % tokens
    offset = key - query
    low = -pos_ref[...]
    masks = [(offset <= 0) & (offset >= low)]
    for step in range(1, back + 1):
        masks.append(offset - step * tokens >= low)
    return masks


def stack_heads(ref, group):
    return jnp.concatenate(
        [
            ref[:, (group * GROUP + m) * HEAD_DIM : (group * GROUP + m + 1) * HEAD_DIM]
            for m in range(GROUP)
        ],
        axis=0,
    )


def key_value(ref, group):
    key = ref[:, group * HEAD_DIM : (group + 1) * HEAD_DIM]
    value = ref[:, KEY_COLUMNS + group * HEAD_DIM : KEY_COLUMNS + (group + 1) * HEAD_DIM]
    return key, value


def attend_forward_kernel(back, pos_ref, q_ref, *refs):
    kv_refs = refs[: back + 1]
    out_ref, inverse_ref = refs[back + 1 :]
    tokens = q_ref.shape[0]
    masks = block_masks(back, tokens, pos_ref)
    inverse_ref[...] = jnp.zeros_like(inverse_ref)
    for group in range(KEY_VALUE_HEADS):
        queries = stack_heads(q_ref, group)
        total = jnp.zeros((1, GROUP * tokens), f32)
        summed = jnp.zeros((HEAD_DIM, GROUP * tokens), f32)
        for step in range(back + 1):
            key, value = key_value(kv_refs[step], group)
            exponent = jnp.where(masks[step], jnp.exp(dot_nt(key, queries)), 0.0)
            total = total + jnp.sum(exponent, axis=0, keepdims=True)
            summed = summed + dot_tn(value, exponent.astype(bf16))
        inverse = 1.0 / total
        inverse_ref[group : group + 1, :] = inverse
        heads = summed * inverse
        for m in range(GROUP):
            head = group * GROUP + m
            out_ref[:, head * HEAD_DIM : (head + 1) * HEAD_DIM] = (
                heads[:, m * tokens : (m + 1) * tokens].T.astype(bf16)
            )


def attend_backward_kernel(back, pos_ref, q_ref, do_ref, inverse_ref, *refs):
    kv_refs = refs[: back + 1]
    dq_ref = refs[back + 1]
    dkv_refs = refs[back + 2 :]
    tokens = q_ref.shape[0]
    masks = block_masks(back, tokens, pos_ref)
    for group in range(KEY_VALUE_HEADS):
        queries = stack_heads(q_ref, group)
        out_grads = stack_heads(do_ref, group)
        inverse = inverse_ref[group : group + 1, :]
        chances, chance_grads = [], []
        row_dot = jnp.zeros((1, GROUP * tokens), f32)
        for step in range(back + 1):
            key, value = key_value(kv_refs[step], group)
            chance = jnp.where(masks[step], jnp.exp(dot_nt(key, queries)) * inverse, 0.0)
            chance_grad = dot_nt(value, out_grads)
            row_dot = row_dot + jnp.sum(chance * chance_grad, axis=0, keepdims=True)
            chances.append(chance)
            chance_grads.append(chance_grad)
        query_grad = jnp.zeros((HEAD_DIM, GROUP * tokens), f32)
        for step in range(back + 1):
            key, _ = key_value(kv_refs[step], group)
            score_grad = (chances[step] * (chance_grads[step] - row_dot)).astype(bf16)
            target = dkv_refs[step]
            target[:, group * HEAD_DIM : (group + 1) * HEAD_DIM] = dot_nn(
                score_grad, queries
            ).astype(target.dtype)
            target[:, KEY_COLUMNS + group * HEAD_DIM : KEY_COLUMNS + (group + 1) * HEAD_DIM] = (
                dot_nn(chances[step].astype(bf16), out_grads).astype(target.dtype)
            )
            query_grad = query_grad + dot_tn(key, score_grad)
        for m in range(GROUP):
            head = group * GROUP + m
            dq_ref[:, head * HEAD_DIM : (head + 1) * HEAD_DIM] = query_grad[
                :, m * tokens : (m + 1) * tokens
            ].T


def ffn_dz_kernel(count, offsets, grads_ref, *refs):
    blocks, out_ref = refs[:-1], refs[-1]
    total = jnp.zeros(out_ref.shape, f32)
    for i, column, piece in pieces_of(blocks, offsets, count):
        total = total + dot_nn(grads_ref[:, column], piece[...])
    out_ref[...] = total


def ffn_mid_kernel(count, offsets, mid_ref, dz_ref, *refs):
    blocks = len(refs) // 2 - 2
    gates, ups = refs[:blocks], refs[blocks : 2 * blocks]
    hidden_ref, gate_grad_ref, up_grad_ref, out_ref = refs[2 * blocks :]
    gate = jnp.zeros(dz_ref.shape, f32)
    up = jnp.zeros(dz_ref.shape, f32)
    for i, column, piece in pieces_of(gates, offsets, count):
        gate = gate + dot_nn(mid_ref[:, column], piece[...])
    for i, column, piece in pieces_of(ups, offsets, count):
        up = up + dot_nn(mid_ref[:, column], piece[...])
    sigmoid = 1.0 / (1.0 + jnp.exp(-gate))
    activated = gate * sigmoid
    hidden_ref[...] = (activated * up).astype(bf16)
    hidden_grad = dz_ref[...]
    slope = sigmoid * (1.0 + gate * (1.0 - sigmoid))
    gate_grad = (hidden_grad * up * slope).astype(bf16)
    up_grad = (hidden_grad * activated).astype(bf16)
    gate_grad_ref[...] = gate_grad
    up_grad_ref[...] = up_grad
    up_pieces = list(pieces_of(ups, offsets, count))
    for i, column, piece in pieces_of(gates, offsets, count):
        out_ref[:, column] = (
            dot_nt(gate_grad, piece[...]) + dot_nt(up_grad, up_pieces[i][2][...])
        ).astype(bf16)


def ffn_out_kernel(count, offsets, hidden_ref, *refs):
    blocks, out_ref = refs[:-1], refs[-1]
    for i, column, piece in pieces_of(blocks, offsets, count):
        out_ref[:, column] = dot_nt(hidden_ref[...], piece[...]).astype(bf16)


def weight_grad_kernel(rows_ref, columns_ref, out_ref):
    out_ref[...] = dot_tn(rows_ref[...], columns_ref[...]).astype(bf16)


def weight_grad(row_side, column_side, name):
    tokens, model = row_side.shape
    width = column_side.shape[1]
    ny, nc, nzh = lax.axis_size("y"), lax.axis_size("core"), lax.axis_size("zh")
    rows = model // (ny * nc * nzh)

    def put(r):
        y, rest = r // (nc * nzh), r % (nc * nzh)
        return ((y * nzh + rest % nzh) * nc + rest // nzh, 0)

    return pl.pallas_call(
        weight_grad_kernel,
        out_shape=jax.ShapeDtypeStruct((model, width), bf16),
        grid=(model // rows,),
        in_specs=[
            pl.BlockSpec((tokens, rows), lambda r: (0, r)),
            pl.BlockSpec((tokens, width), lambda r: (0, 0)),
        ],
        out_specs=pl.BlockSpec((rows, width), put),
        name=name,
        compiler_params=pltpu.CompilerParams(vmem_limit_bytes=32 << 20),
        cost_estimate=pl.CostEstimate(
            flops=2 * tokens * model * width,
            transcendentals=0,
            bytes_accessed=2 * (tokens * model + tokens * width + model * width),
        ),
    )(row_side, column_side)


def pieces_of(blocks, offsets, count):
    i = 0
    for block in blocks:
        rows = block.shape[0] // count
        for c in range(count):
            column = pl.ds(pl.multiple_of(offsets[i], 128), rows)
            yield i, column, block.at[c * rows : (c + 1) * rows, :]
            i += 1


def by_tokens(kernel, offsets, token_arrays, blocks, outs, name, flops):
    tokens = token_arrays[0].shape[0]
    chunk = min(256, tokens)
    blocks = [block.reshape(-1, block.shape[-1]) for block in blocks]
    moved = 2 * sum(b.size for b in blocks) + 2 * sum(t.size for t in token_arrays)
    row = lambda width: pl.BlockSpec((chunk, width), lambda t, o: (t, 0))
    return pl.pallas_call(
        functools.partial(kernel, lax.axis_size("core")),
        out_shape=tuple(jax.ShapeDtypeStruct((tokens, width), kind) for width, kind in outs),
        grid_spec=pltpu.PrefetchScalarGridSpec(
            num_scalar_prefetch=1,
            grid=(tokens // chunk,),
            in_specs=[row(t.shape[1]) for t in token_arrays]
            + [pl.BlockSpec(b.shape, lambda t, o: (0, 0)) for b in blocks],
            out_specs=tuple(row(width) for width, _ in outs),
        ),
        name=name,
        compiler_params=pltpu.CompilerParams(vmem_limit_bytes=48 << 20),
        cost_estimate=pl.CostEstimate(flops=flops, transcendentals=0, bytes_accessed=moved),
    )(offsets, *token_arrays, *blocks)


def whole(kernel, out_shapes, name, flops, moved):
    return pl.pallas_call(
        kernel,
        out_shape=out_shapes,
        name=name,
        compiler_params=pltpu.CompilerParams(vmem_limit_bytes=48 << 20),
        cost_estimate=pl.CostEstimate(flops=flops, transcendentals=0, bytes_accessed=moved),
    )


def swap(value, axis, k):
    n = lax.axis_size(axis)
    return lax.ppermute(value, axis, [(i, i ^ k) for i in range(n)])


def shifted(value, step):
    n = lax.axis_size(SEQ)
    return lax.ppermute(value, SEQ, [(i, i + step) for i in range(n) if 0 <= i + step < n])


def tie(*values):
    return lax.optimization_barrier(values)


def team_columns(pieces):
    team, nc = lax.axis_size(TEAM), lax.axis_size("core")
    rows = pieces[0].shape[0]
    blocks = jnp.concatenate([p.reshape(rows, team, -1) for p in pieces], axis=2)
    blocks = lax.all_to_all(blocks.transpose(1, 0, 2), TEAM, 0, 0, tiled=True)
    return blocks.reshape(1, nc, 1, -1, blocks.shape[2])


def exchange(block, axis):
    return [block] + [swap(block, axis, k) for k in range(1, lax.axis_size(axis))]


def place(pieces):
    y, zh = lax.axis_index("y"), lax.axis_index("zh")
    _, nc, _, rest, width = pieces[0][0].shape
    full = jnp.zeros((lax.axis_size("y"), nc, lax.axis_size("zh"), rest, width), bf16)
    for b, row in enumerate(pieces):
        for a, piece in enumerate(row):
            full = lax.dynamic_update_slice(full, piece, (y ^ a, 0, zh ^ b, 0, 0))
    return full.reshape(-1, width)


def reduce_y(partial):
    y = lax.axis_index("y")
    total = lax.dynamic_index_in_dim(partial, y, 0, keepdims=False).astype(f32)
    for a in range(1, lax.axis_size("y")):
        total = total + swap(
            lax.dynamic_index_in_dim(partial, y ^ a, 0, keepdims=False), "y", a
        ).astype(f32)
    return total


def reduce_zh(total):
    zh = lax.axis_index("zh")
    out = lax.dynamic_index_in_dim(total, zh, 1, keepdims=False)
    for b in range(1, lax.axis_size("zh")):
        out = out + swap(
            lax.dynamic_index_in_dim(total, zh ^ b, 1, keepdims=False).astype(bf16), "zh", b
        ).astype(f32)
    return out


def return_columns(totals):
    team = lax.axis_size(TEAM)
    parts = [total.astype(bf16).reshape(team, -1, total.shape[-1]) for total in totals]
    blocks = lax.all_to_all(jnp.concatenate(parts, axis=2), TEAM, 0, 0, tiled=True)
    grads, start = [], 0
    for part in parts:
        width = part.shape[2]
        grad = blocks[:, :, start : start + width].transpose(1, 0, 2)
        grads.append(grad.reshape(grad.shape[0], -1).astype(f32))
        start += width
    return grads


def team_core(partial):
    nc = lax.axis_size("core")
    core = lax.axis_index("core")
    halves = partial.reshape(nc, -1, partial.shape[1])
    total = lax.dynamic_index_in_dim(halves, core, 0, keepdims=False).astype(f32)
    for k in range(1, nc):
        total = total + swap(
            lax.dynamic_index_in_dim(halves, core ^ k, 0, keepdims=False), "core", k
        ).astype(f32)
    return total.astype(bf16)


def team_chips(total):
    chips, chip = lax.axis_size(CHIPS), lax.axis_index(CHIPS)
    blocks = total.reshape(chips, -1, total.shape[1])
    block = lambda i: lax.dynamic_index_in_dim(blocks, i, 0, keepdims=False)
    far = [
        lax.ppermute(block(chip ^ k), CHIPS, [(i, i ^ k) for i in range(chips)])
        for k in range(1, chips)
    ]
    out = block(chip).astype(f32)
    for piece in far:
        out = out + piece.astype(f32)
    return out


def team_sum(partial):
    return team_chips(team_core(partial))


def row_team(value):
    tokens = value.shape[0]
    ny, nc, nzh = lax.axis_size("y"), lax.axis_size("core"), lax.axis_size("zh")
    chips, team = lax.axis_size(CHIPS), lax.axis_size(TEAM)
    split = value.reshape(tokens, ny, nc, nzh, chips, -1).transpose(2, 4, 0, 1, 3, 5)
    split = split.reshape(team, tokens, -1)
    return lax.all_to_all(split, TEAM, 0, 0, tiled=True).reshape(team * tokens, -1)


def own_rows(value):
    ny, nc, nzh = lax.axis_size("y"), lax.axis_size("core"), lax.axis_size("zh")
    split = value.reshape(value.shape[0], ny, nc, nzh, lax.axis_size(CHIPS), -1)
    split = lax.dynamic_index_in_dim(split, lax.axis_index("core"), 2, keepdims=False)
    split = lax.dynamic_index_in_dim(split, lax.axis_index(CHIPS), 3, keepdims=False)
    return split.reshape(value.shape[0], -1)


def sum_over(value, axes):
    for axis in axes:
        k = 1
        while k < lax.axis_size(axis):
            value = value + swap(value, axis, k)
            k *= 2
    return value


def local(
    layer_input,
    segments,
    positions,
    query_key_value_weight,
    w_out,
    w_gate,
    w_up,
    w_down,
    g_attn,
    g_ffn,
    g_query,
    g_key,
    cotangent,
):
    tokens, model = layer_input.shape
    back = lax.axis_size(SEQ) // 2
    ff = w_gate.shape[1] // lax.axis_size(TEAM)

    inputs = layer_input.astype(f32)
    scale_in = row_scale(inputs)
    normed_in = inputs * scale_in
    normed_low = (normed_in * g_attn).astype(bf16)

    team = lax.axis_size(TEAM)
    joined_columns = query_key_value_weight.shape[1]
    padded = -(-joined_columns // (128 * team)) * 128 * team

    y, zh = lax.axis_index("y"), lax.axis_index("zh")
    ny, nc, nzh = lax.axis_size("y"), lax.axis_size("core"), lax.axis_size("zh")
    width = model // (ny * nc * nzh)
    offsets = jnp.stack(
        [
            (((y ^ a) * nc + c) * nzh + (zh ^ b)) * width
            for b in range(nzh)
            for a in range(ny)
            for c in range(nc)
        ]
    ).astype(jnp.int32)

    normed_team = lax.all_gather(normed_low, TEAM, axis=0, tiled=True)
    qkv_block = team_columns([jnp.pad(query_key_value_weight, ((0, 0), (0, padded - joined_columns)))])
    qkv_block, w_down, w_out = tie(qkv_block, w_down, w_out)
    qkv_near, qkv_far = exchange(qkv_block, "y"), exchange(qkv_block, "zh")
    out_near = exchange(w_out[None, None], "zh")
    down_block = team_columns([w_down])
    out_part = [exchange(piece, "y") for piece in out_near]
    qkv_part = place([qkv_near] + [exchange(piece, "y") for piece in qkv_far[1:]])
    out_rows = jnp.zeros((ny, nzh) + w_out.shape, bf16)
    for b, row in enumerate(out_part):
        for a, piece in enumerate(row):
            out_rows = lax.dynamic_update_slice(out_rows, piece, (y ^ a, zh ^ b, 0, 0))

    normed_team, qkv_part, out_rows, down_block, w_gate = tie(
        normed_team, qkv_part, out_rows, down_block, w_gate
    )
    out_full = lax.all_gather(out_rows, TEAM, axis=0, tiled=False)
    out_full = (
        out_full.reshape((nc, lax.axis_size(CHIPS)) + out_rows.shape)
        .transpose(2, 0, 3, 1, 4, 5)
        .reshape(model, -1)
    )
    down_far, down_near = exchange(down_block, "zh"), exchange(down_block, "y")
    joined_team = dot_nn(normed_team, qkv_part).astype(bf16)
    joined = lax.all_to_all(
        joined_team.reshape(team, tokens, -1), TEAM, 0, 0, tiled=True
    )
    joined, w_gate, w_up, down_near = tie(joined, w_gate, w_up, down_near)
    gate_up_block = team_columns([w_gate, w_up])

    half = HEAD_DIM // 2
    frequency = 10000.0 ** (-jnp.arange(half, dtype=f32) / half)
    angles = positions.astype(f32)[:, None] * frequency[None, :]
    angles = jnp.concatenate([angles, angles], axis=-1)
    cosine, sine = jnp.cos(angles), jnp.sin(angles)
    gq, gk = g_query[None, :], g_key[None, :]
    query_low, kv_low = whole(
        heads_forward_kernel,
        (
            jax.ShapeDtypeStruct((tokens, QUERY_COLUMNS), bf16),
            jax.ShapeDtypeStruct((tokens, 2 * KEY_COLUMNS), bf16),
        ),
        "heads_forward",
        tokens * 1920 * 20,
        tokens * 1920 * 6,
    )(joined, cosine, sine, gq, gk)

    kv_blocks = [kv_low] + [shifted(kv_low, step) for step in range(1, back + 1)]
    kv_blocks, down_far, gate_up_block, cotangent_in = tie(
        kv_blocks, down_far, gate_up_block, cotangent
    )
    gate_block, up_block = gate_up_block[..., :ff], gate_up_block[..., ff:]
    gate_far = exchange(gate_block, "zh")
    grads_out = lax.all_gather(cotangent_in, TEAM, axis=0, tiled=True)
    tiled_positions = jnp.tile(positions[None, :], (1, GROUP))
    attended, inverse = whole(
        functools.partial(attend_forward_kernel, back),
        (
            jax.ShapeDtypeStruct((tokens, QUERY_COLUMNS), bf16),
            jax.ShapeDtypeStruct((8, GROUP * tokens), f32),
        ),
        "attend_forward",
        4 * tokens * tokens * (back + 1) * QUERY_COLUMNS,
        tokens * 2000 * 10,
    )(tiled_positions, query_low, *kv_blocks)

    gate_near = exchange(gate_block, "y")
    down_blocks = down_near + sum([exchange(piece, "y") for piece in down_far[1:]], [])
    attended, out_full, gate_far, up_block, gate_near, down_blocks = tie(
        attended, out_full, gate_far, up_block, gate_near, down_blocks
    )
    up_far, up_near = exchange(up_block, "zh"), exchange(up_block, "y")
    gate_blocks = gate_near + sum([exchange(piece, "y") for piece in gate_far[1:]], [])
    middle = inputs + dot_nt(attended, out_full)
    scale_mid = row_scale(middle)
    normed_mid = middle * scale_mid
    mid_low = (normed_mid * g_ffn).astype(bf16)
    mid_team = lax.all_gather(mid_low, TEAM, axis=0, tiled=True)

    products = 2 * mid_team.shape[0] * model * ff
    up_blocks = up_near + sum([exchange(piece, "y") for piece in up_far[1:]], [])
    (hidden_grad,) = by_tokens(
        ffn_dz_kernel, offsets, [grads_out], down_blocks, [(ff, f32)], "ffn_dz", products
    )
    hidden_grad, gate_blocks, up_blocks = tie(hidden_grad, gate_blocks, up_blocks)
    mid_team, hidden_grad, attended_in = tie(mid_team, hidden_grad, attended)
    attended_team = lax.all_gather(attended_in, TEAM, axis=0, tiled=True)
    hidden, gate_grad, up_grad, mid_part = by_tokens(
        ffn_mid_kernel,
        offsets,
        [mid_team, hidden_grad],
        gate_blocks + up_blocks,
        [(ff, bf16), (ff, bf16), (ff, bf16), (model, bf16)],
        "ffn_mid",
        4 * products,
    )

    scatter = lambda part: lax.psum_scatter(part, ("y", "zh"), scatter_dimension=0, tiled=True)
    mid_part, attended_team, hidden = tie(mid_part, attended_team, hidden)
    mid_half = team_core(mid_part)
    down_part = weight_grad(grads_out, hidden, "down_grad")
    down_sum = scatter(down_part)
    mid_half, hidden, _ = tie(mid_half, hidden, down_part)
    mid_grad = team_chips(mid_half)
    branch_half = team_core(
        by_tokens(
            ffn_out_kernel, offsets, [hidden], down_blocks, [(model, bf16)], "ffn_out", products
        )[0]
    )
    mid_grad, branch_half, mid_team, gate_grad, up_grad = tie(
        mid_grad, branch_half, mid_team, gate_grad, up_grad
    )

    weighted = mid_grad * g_ffn
    ffn_gain = jnp.sum(mid_grad * normed_mid, axis=0)
    middle_grad = cotangent.astype(f32) + scale_mid * (
        weighted - normed_mid * jnp.mean(weighted * normed_mid, axis=-1, keepdims=True)
    )
    branch_grad = middle_grad.astype(bf16)
    head_grads = dot_nn(branch_grad, out_full).astype(bf16)
    results = whole(
        functools.partial(attend_backward_kernel, back),
        (
            jax.ShapeDtypeStruct((tokens, QUERY_COLUMNS), f32),
            jax.ShapeDtypeStruct((tokens, 2 * KEY_COLUMNS), f32),
        )
        + (jax.ShapeDtypeStruct((tokens, 2 * KEY_COLUMNS), bf16),) * back,
        "attend_backward",
        10 * tokens * tokens * (back + 1) * QUERY_COLUMNS,
        tokens * 2000 * 20,
    )(tiled_positions, query_low, head_grads, inverse, *kv_blocks)
    query_grad, own_grad, far_grads = results[0], results[1], results[2:]
    far_grads, gate_grad, mid_team_in = tie(far_grads, gate_grad, mid_team)
    gate_part = weight_grad(mid_team_in, gate_grad, "gate_grad")
    received = [shifted(grad, -(i + 1)) for i, grad in enumerate(far_grads)]
    received, down_sum, gate_part, up_grad = tie(received, down_sum, gate_part, up_grad)
    gate_sum = scatter(gate_part)
    joined_grad, head_gains = whole(
        functools.partial(heads_backward_kernel, back),
        (
            jax.ShapeDtypeStruct(joined.shape, bf16),
            jax.ShapeDtypeStruct((1, 2 * HEAD_DIM), f32),
        ),
        "heads_backward",
        tokens * 1920 * 30,
        tokens * 1920 * 16,
    )(joined, cosine, sine, gq, gk, query_grad, own_grad, *received)

    joined_grad, up_grad, mid_team = tie(joined_grad, up_grad, mid_team)
    up_part = weight_grad(mid_team, up_grad, "up_grad")
    joined_grad = lax.all_to_all(joined_grad, TEAM, 0, 0, tiled=True).reshape(-1, padded // team)
    joined_grad, up_part, down_sum = tie(joined_grad, up_part, down_sum)
    up_sum = scatter(up_part)
    normed_half = team_core(dot_nt(joined_grad, qkv_part).astype(bf16))
    normed_half, branch_grad = tie(normed_half, branch_grad)
    normed_in_grad = team_chips(normed_half)
    branch_rows = row_team(branch_grad)
    normed_in_grad, gate_sum, joined_grad, down_sum, branch_rows, branch_half = tie(
        normed_in_grad, gate_sum, joined_grad, down_sum, branch_rows, branch_half
    )
    qkv_sum = reduce_zh(
        reduce_y(
            dot_tn(normed_team, joined_grad).astype(bf16).reshape(ny, nc, nzh, -1, padded // team)
        )
    )
    w_down_grad, w_gate_grad = return_columns([down_sum, gate_sum])
    out_part = dot_tn(branch_rows, attended_team).astype(bf16)
    out_sum = reduce_y(out_part.reshape(ny, 1, nzh, -1, out_part.shape[1]))
    branch_two = team_chips(branch_half)
    weighted_in = normed_in_grad * g_attn
    attn_gain = jnp.sum(normed_in_grad * normed_in, axis=0)
    input_grad = (
        middle_grad
        + scale_in
        * (weighted_in - normed_in * jnp.mean(weighted_in * normed_in, axis=-1, keepdims=True))
    ).astype(bf16)

    gains = sum_over(
        jnp.concatenate([attn_gain, ffn_gain, head_gains[0]], axis=0).reshape(-1, 128),
        ("core", "x"),
    )
    gains, up_sum, qkv_sum, out_sum, branch_two = tie(
        gains, up_sum, qkv_sum, out_sum, branch_two
    )
    w_up_grad, w_qkv_grad = return_columns([up_sum, qkv_sum])
    w_qkv_grad = w_qkv_grad[:, :joined_columns]
    gains = sum_over(gains, ("y", "zl", "zh")).reshape(-1)
    w_out_grad = reduce_zh(out_sum).reshape(-1, out_sum.shape[-1])
    result = (middle + branch_two).astype(bf16)
    return (
        result,
        input_grad,
        w_qkv_grad,
        w_out_grad,
        w_gate_grad,
        w_up_grad,
        w_down_grad,
        gains[:model],
        gains[model : 2 * model],
        gains[2 * model : 2 * model + HEAD_DIM],
        gains[2 * model + HEAD_DIM :],
    )


def solution(mesh):
    inner, outer = mesh.devices.shape
    split = Mesh(mesh.devices.reshape(inner // 2, 2, 2, 2, outer // 4), ALL)
    rows, whole_array = P(ALL, None), P()
    in_specs = (rows, P(ALL), P(ALL)) + (rows,) * 5 + (whole_array,) * 4 + (rows,)
    out_specs = (rows,) * 7 + (whole_array,) * 4
    return jax.shard_map(local, mesh=split, in_specs=in_specs, out_specs=out_specs, check_vma=False)
```

```python
import functools

import jax
import jax.numpy as jnp
from jax import lax
from jax.experimental import pallas as pl
from jax.experimental.pallas import tpu as pltpu
from jax.sharding import Mesh
from jax.sharding import PartitionSpec as P

QUERY_HEADS = 20
KEY_VALUE_HEADS = 5
HEAD_DIM = 64
GROUP = QUERY_HEADS // KEY_VALUE_HEADS
QUERY_COLUMNS = QUERY_HEADS * HEAD_DIM
KEY_COLUMNS = KEY_VALUE_HEADS * HEAD_DIM
NORM_EPS = 1e-06

ALL = ("y", "core", "zh", "zl", "x")
SEQ = ("zh", "zl", "x")
TEAM = ("core", "zl", "x")
CHIPS = ("zl", "x")

bf16 = jnp.bfloat16
f32 = jnp.float32


def dot_nn(left, right):
    return jnp.dot(left, right, preferred_element_type=f32)


def dot_nt(left, right):
    return lax.dot_general(left, right, (((1,), (1,)), ((), ())), preferred_element_type=f32)


def dot_tn(left, right):
    return lax.dot_general(left, right, (((0,), (0,)), ((), ())), preferred_element_type=f32)


def row_scale(values):
    return lax.rsqrt(jnp.mean(values * values, axis=-1, keepdims=True) + NORM_EPS)


def head_norm(values):
    scale = lax.rsqrt(jnp.mean(values * values, axis=-1, keepdims=True) + NORM_EPS)
    return values * scale, scale


def turn(values):
    half = HEAD_DIM // 2
    return jnp.concatenate([-values[:, half:], values[:, :half]], axis=1)


def turn_back(values):
    half = HEAD_DIM // 2
    return jnp.concatenate([values[:, half:], -values[:, :half]], axis=1)


def block_head(ref, head):
    block, start = divmod(head * HEAD_DIM, ref.shape[2])
    return ref[block, :, start : start + HEAD_DIM].astype(f32)


def block_store(ref, head, value):
    block, start = divmod(head * HEAD_DIM, ref.shape[2])
    ref[block, :, start : start + HEAD_DIM] = value


def heads_forward_kernel(qkv_ref, cos_ref, sin_ref, gq_ref, gk_ref, q_ref, kv_ref):
    cosine, sine = cos_ref[...], sin_ref[...]
    for head in range(QUERY_HEADS + KEY_VALUE_HEADS):
        columns = slice(head * HEAD_DIM, (head + 1) * HEAD_DIM)
        normed, _ = head_norm(block_head(qkv_ref, head))
        if head < QUERY_HEADS:
            scaled = normed * gq_ref[...]
            turned = (scaled * cosine + turn(scaled) * sine) * (HEAD_DIM**-0.5)
            q_ref[:, columns] = turned.astype(bf16)
        else:
            scaled = normed * gk_ref[...]
            turned = scaled * cosine + turn(scaled) * sine
            place = slice((head - QUERY_HEADS) * HEAD_DIM, (head - QUERY_HEADS + 1) * HEAD_DIM)
            kv_ref[:, place] = turned.astype(bf16)
    for head in range(KEY_VALUE_HEADS):
        place = slice(KEY_COLUMNS + head * HEAD_DIM, KEY_COLUMNS + (head + 1) * HEAD_DIM)
        value = block_head(qkv_ref, QUERY_HEADS + KEY_VALUE_HEADS + head)
        kv_ref[:, place] = value.astype(bf16)


def heads_backward_kernel(
    back, qkv_ref, cos_ref, sin_ref, gq_ref, gk_ref, dq_ref, own_ref, *refs
):
    received = refs[:back]
    grad_ref, gain_ref = refs[back:]
    cosine, sine = cos_ref[...], sin_ref[...]
    kv_grad = own_ref[...]
    for piece in received:
        kv_grad = kv_grad + piece[...].astype(f32)
    totals = [jnp.zeros((1, HEAD_DIM), f32), jnp.zeros((1, HEAD_DIM), f32)]
    for head in range(QUERY_HEADS + KEY_VALUE_HEADS):
        columns = slice(head * HEAD_DIM, (head + 1) * HEAD_DIM)
        normed, scale = head_norm(block_head(qkv_ref, head))
        is_key = int(head >= QUERY_HEADS)
        if is_key:
            place = slice((head - QUERY_HEADS) * HEAD_DIM, (head - QUERY_HEADS + 1) * HEAD_DIM)
            grad = kv_grad[:, place]
            gain = gk_ref[...]
        else:
            grad = dq_ref[:, columns] * (HEAD_DIM**-0.5)
            gain = gq_ref[...]
        grad = grad * cosine + turn_back(grad * sine)
        totals[is_key] = totals[is_key] + jnp.sum(grad * normed, axis=0, keepdims=True)
        weighted = grad * gain
        inner = jnp.mean(weighted * normed, axis=-1, keepdims=True)
        block_store(grad_ref, head, (scale * (weighted - normed * inner)).astype(bf16))
    for head in range(KEY_VALUE_HEADS):
        place = slice(KEY_COLUMNS + head * HEAD_DIM, KEY_COLUMNS + (head + 1) * HEAD_DIM)
        block_store(grad_ref, QUERY_HEADS + KEY_VALUE_HEADS + head, kv_grad[:, place].astype(bf16))
    count, tokens, width = grad_ref.shape
    for head in range(QUERY_HEADS + 2 * KEY_VALUE_HEADS, count * width // HEAD_DIM):
        block_store(grad_ref, head, jnp.zeros((tokens, HEAD_DIM), bf16))
    gain_ref[...] = jnp.concatenate(totals, axis=1)


def block_masks(back, tokens, pos_ref):
    key = lax.broadcasted_iota(jnp.int32, (tokens, GROUP * tokens), 0)
    query = lax.broadcasted_iota(jnp.int32, (tokens, GROUP * tokens), 1) % tokens
    offset = key - query
    low = -pos_ref[...]
    masks = [(offset <= 0) & (offset >= low)]
    for step in range(1, back + 1):
        masks.append(offset - step * tokens >= low)
    return masks


def stack_heads(ref, group):
    return jnp.concatenate(
        [
            ref[:, (group * GROUP + m) * HEAD_DIM : (group * GROUP + m + 1) * HEAD_DIM]
            for m in range(GROUP)
        ],
        axis=0,
    )


def key_value(ref, group):
    key = ref[:, group * HEAD_DIM : (group + 1) * HEAD_DIM]
    value = ref[:, KEY_COLUMNS + group * HEAD_DIM : KEY_COLUMNS + (group + 1) * HEAD_DIM]
    return key, value


def attend_forward_kernel(back, pos_ref, q_ref, *refs):
    kv_refs = refs[: back + 1]
    out_ref, inverse_ref = refs[back + 1 :]
    tokens = q_ref.shape[0]
    masks = block_masks(back, tokens, pos_ref)
    inverse_ref[...] = jnp.zeros_like(inverse_ref)
    for group in range(KEY_VALUE_HEADS):
        queries = stack_heads(q_ref, group)
        total = jnp.zeros((1, GROUP * tokens), f32)
        summed = jnp.zeros((HEAD_DIM, GROUP * tokens), f32)
        for step in range(back + 1):
            key, value = key_value(kv_refs[step], group)
            exponent = jnp.where(masks[step], jnp.exp(dot_nt(key, queries)), 0.0)
            total = total + jnp.sum(exponent, axis=0, keepdims=True)
            summed = summed + dot_tn(value, exponent.astype(bf16))
        inverse = 1.0 / total
        inverse_ref[group : group + 1, :] = inverse
        heads = summed * inverse
        for m in range(GROUP):
            head = group * GROUP + m
            out_ref[:, head * HEAD_DIM : (head + 1) * HEAD_DIM] = (
                heads[:, m * tokens : (m + 1) * tokens].T.astype(bf16)
            )


def attend_backward_kernel(back, pos_ref, q_ref, do_ref, inverse_ref, *refs):
    kv_refs = refs[: back + 1]
    dq_ref = refs[back + 1]
    dkv_refs = refs[back + 2 :]
    tokens = q_ref.shape[0]
    masks = block_masks(back, tokens, pos_ref)
    for group in range(KEY_VALUE_HEADS):
        queries = stack_heads(q_ref, group)
        out_grads = stack_heads(do_ref, group)
        inverse = inverse_ref[group : group + 1, :]
        chances, chance_grads = [], []
        row_dot = jnp.zeros((1, GROUP * tokens), f32)
        for step in range(back + 1):
            key, value = key_value(kv_refs[step], group)
            chance = jnp.where(masks[step], jnp.exp(dot_nt(key, queries)) * inverse, 0.0)
            chance_grad = dot_nt(value, out_grads)
            row_dot = row_dot + jnp.sum(chance * chance_grad, axis=0, keepdims=True)
            chances.append(chance)
            chance_grads.append(chance_grad)
        query_grad = jnp.zeros((HEAD_DIM, GROUP * tokens), f32)
        for step in range(back + 1):
            key, _ = key_value(kv_refs[step], group)
            score_grad = (chances[step] * (chance_grads[step] - row_dot)).astype(bf16)
            target = dkv_refs[step]
            target[:, group * HEAD_DIM : (group + 1) * HEAD_DIM] = dot_nn(
                score_grad, queries
            ).astype(target.dtype)
            target[:, KEY_COLUMNS + group * HEAD_DIM : KEY_COLUMNS + (group + 1) * HEAD_DIM] = (
                dot_nn(chances[step].astype(bf16), out_grads).astype(target.dtype)
            )
            query_grad = query_grad + dot_tn(key, score_grad)
        for m in range(GROUP):
            head = group * GROUP + m
            dq_ref[:, head * HEAD_DIM : (head + 1) * HEAD_DIM] = query_grad[
                :, m * tokens : (m + 1) * tokens
            ].T


def ffn_dz_kernel(count, offsets, grads_ref, *refs):
    blocks, out_ref = refs[:-1], refs[-1]
    total = jnp.zeros(out_ref.shape, f32)
    for i, column, piece in pieces_of(blocks, offsets, count):
        total = total + dot_nn(grads_ref[:, column], piece[...])
    out_ref[...] = total


def ffn_mid_kernel(count, offsets, mid_ref, dz_ref, *refs):
    blocks = len(refs) // 2 - 2
    gates, ups = refs[:blocks], refs[blocks : 2 * blocks]
    hidden_ref, gate_grad_ref, up_grad_ref, out_ref = refs[2 * blocks :]
    gate = jnp.zeros(dz_ref.shape, f32)
    up = jnp.zeros(dz_ref.shape, f32)
    for i, column, piece in pieces_of(gates, offsets, count):
        gate = gate + dot_nn(mid_ref[:, column], piece[...])
    for i, column, piece in pieces_of(ups, offsets, count):
        up = up + dot_nn(mid_ref[:, column], piece[...])
    sigmoid = 1.0 / (1.0 + jnp.exp(-gate))
    activated = gate * sigmoid
    hidden_ref[...] = (activated * up).astype(bf16)
    hidden_grad = dz_ref[...]
    slope = sigmoid * (1.0 + gate * (1.0 - sigmoid))
    gate_grad = (hidden_grad * up * slope).astype(bf16)
    up_grad = (hidden_grad * activated).astype(bf16)
    gate_grad_ref[...] = gate_grad
    up_grad_ref[...] = up_grad
    up_pieces = list(pieces_of(ups, offsets, count))
    for i, column, piece in pieces_of(gates, offsets, count):
        out_ref[:, column] = (
            dot_nt(gate_grad, piece[...]) + dot_nt(up_grad, up_pieces[i][2][...])
        ).astype(bf16)


def ffn_out_kernel(count, offsets, hidden_ref, *refs):
    blocks, out_ref = refs[:-1], refs[-1]
    for i, column, piece in pieces_of(blocks, offsets, count):
        out_ref[:, column] = dot_nt(hidden_ref[...], piece[...]).astype(bf16)


def weight_grad_kernel(rows_ref, columns_ref, out_ref):
    out_ref[...] = dot_tn(rows_ref[...], columns_ref[...]).astype(bf16)


def weight_grad(row_side, column_side, name):
    tokens, model = row_side.shape
    width = column_side.shape[1]
    ny, nc, nzh = lax.axis_size("y"), lax.axis_size("core"), lax.axis_size("zh")
    rows = model // (ny * nc * nzh)

    def put(r):
        y, rest = r // (nc * nzh), r % (nc * nzh)
        return ((y * nzh + rest % nzh) * nc + rest // nzh, 0)

    return pl.pallas_call(
        weight_grad_kernel,
        out_shape=jax.ShapeDtypeStruct((model, width), bf16),
        grid=(model // rows,),
        in_specs=[
            pl.BlockSpec((tokens, rows), lambda r: (0, r)),
            pl.BlockSpec((tokens, width), lambda r: (0, 0)),
        ],
        out_specs=pl.BlockSpec((rows, width), put),
        name=name,
        compiler_params=pltpu.CompilerParams(vmem_limit_bytes=32 << 20),
        cost_estimate=pl.CostEstimate(
            flops=2 * tokens * model * width,
            transcendentals=0,
            bytes_accessed=2 * (tokens * model + tokens * width + model * width),
        ),
    )(row_side, column_side)


def pieces_of(blocks, offsets, count):
    i = 0
    for block in blocks:
        rows = block.shape[0] // count
        for c in range(count):
            column = pl.ds(pl.multiple_of(offsets[i], 128), rows)
            yield i, column, block.at[c * rows : (c + 1) * rows, :]
            i += 1


def by_tokens(kernel, offsets, token_arrays, blocks, outs, name, flops):
    tokens = token_arrays[0].shape[0]
    chunk = min(256, tokens)
    blocks = [block.reshape(-1, block.shape[-1]) for block in blocks]
    moved = 2 * sum(b.size for b in blocks) + 2 * sum(t.size for t in token_arrays)
    row = lambda width: pl.BlockSpec((chunk, width), lambda t, o: (t, 0))
    return pl.pallas_call(
        functools.partial(kernel, lax.axis_size("core")),
        out_shape=tuple(jax.ShapeDtypeStruct((tokens, width), kind) for width, kind in outs),
        grid_spec=pltpu.PrefetchScalarGridSpec(
            num_scalar_prefetch=1,
            grid=(tokens // chunk,),
            in_specs=[row(t.shape[1]) for t in token_arrays]
            + [pl.BlockSpec(b.shape, lambda t, o: (0, 0)) for b in blocks],
            out_specs=tuple(row(width) for width, _ in outs),
        ),
        name=name,
        compiler_params=pltpu.CompilerParams(vmem_limit_bytes=48 << 20),
        cost_estimate=pl.CostEstimate(flops=flops, transcendentals=0, bytes_accessed=moved),
    )(offsets, *token_arrays, *blocks)


def whole(kernel, out_shapes, name, flops, moved):
    return pl.pallas_call(
        kernel,
        out_shape=out_shapes,
        name=name,
        compiler_params=pltpu.CompilerParams(vmem_limit_bytes=48 << 20),
        cost_estimate=pl.CostEstimate(flops=flops, transcendentals=0, bytes_accessed=moved),
    )


def swap(value, axis, k):
    n = lax.axis_size(axis)
    return lax.ppermute(value, axis, [(i, i ^ k) for i in range(n)])


def shifted(value, step):
    n = lax.axis_size(SEQ)
    return lax.ppermute(value, SEQ, [(i, i + step) for i in range(n) if 0 <= i + step < n])


def tie(*values):
    return lax.optimization_barrier(values)


def team_columns(pieces):
    team, nc = lax.axis_size(TEAM), lax.axis_size("core")
    rows = pieces[0].shape[0]
    blocks = jnp.concatenate([p.reshape(rows, team, -1) for p in pieces], axis=2)
    blocks = lax.all_to_all(blocks.transpose(1, 0, 2), TEAM, 0, 0, tiled=True)
    return blocks.reshape(1, nc, 1, -1, blocks.shape[2])


def exchange(block, axis):
    return [block] + [swap(block, axis, k) for k in range(1, lax.axis_size(axis))]


def place(pieces):
    y, zh = lax.axis_index("y"), lax.axis_index("zh")
    _, nc, _, rest, width = pieces[0][0].shape
    full = jnp.zeros((lax.axis_size("y"), nc, lax.axis_size("zh"), rest, width), bf16)
    for b, row in enumerate(pieces):
        for a, piece in enumerate(row):
            full = lax.dynamic_update_slice(full, piece, (y ^ a, 0, zh ^ b, 0, 0))
    return full.reshape(-1, width)


def reduce_y(partial):
    y = lax.axis_index("y")
    total = lax.dynamic_index_in_dim(partial, y, 0, keepdims=False).astype(f32)
    for a in range(1, lax.axis_size("y")):
        total = total + swap(
            lax.dynamic_index_in_dim(partial, y ^ a, 0, keepdims=False), "y", a
        ).astype(f32)
    return total


def reduce_zh(total):
    zh = lax.axis_index("zh")
    out = lax.dynamic_index_in_dim(total, zh, 1, keepdims=False)
    for b in range(1, lax.axis_size("zh")):
        out = out + swap(
            lax.dynamic_index_in_dim(total, zh ^ b, 1, keepdims=False).astype(bf16), "zh", b
        ).astype(f32)
    return out


def return_columns(totals):
    team = lax.axis_size(TEAM)
    parts = [total.astype(bf16).reshape(team, -1, total.shape[-1]) for total in totals]
    blocks = lax.all_to_all(jnp.concatenate(parts, axis=2), TEAM, 0, 0, tiled=True)
    grads, start = [], 0
    for part in parts:
        width = part.shape[2]
        grad = blocks[:, :, start : start + width].transpose(1, 0, 2)
        grads.append(grad.reshape(grad.shape[0], -1).astype(f32))
        start += width
    return grads


def team_core(partial):
    nc = lax.axis_size("core")
    core = lax.axis_index("core")
    halves = partial.reshape(nc, -1, partial.shape[1])
    total = lax.dynamic_index_in_dim(halves, core, 0, keepdims=False).astype(f32)
    for k in range(1, nc):
        total = total + swap(
            lax.dynamic_index_in_dim(halves, core ^ k, 0, keepdims=False), "core", k
        ).astype(f32)
    return total.astype(bf16)


def team_chips(total):
    chips, chip = lax.axis_size(CHIPS), lax.axis_index(CHIPS)
    blocks = total.reshape(chips, -1, total.shape[1])
    block = lambda i: lax.dynamic_index_in_dim(blocks, i, 0, keepdims=False)
    far = [
        lax.ppermute(block(chip ^ k), CHIPS, [(i, i ^ k) for i in range(chips)])
        for k in range(1, chips)
    ]
    out = block(chip).astype(f32)
    for piece in far:
        out = out + piece.astype(f32)
    return out


def team_sum(partial):
    return team_chips(team_core(partial))


def row_team(value):
    tokens = value.shape[0]
    ny, nc, nzh = lax.axis_size("y"), lax.axis_size("core"), lax.axis_size("zh")
    chips, team = lax.axis_size(CHIPS), lax.axis_size(TEAM)
    split = value.reshape(tokens, ny, nc, nzh, chips, -1).transpose(2, 4, 0, 1, 3, 5)
    split = split.reshape(team, tokens, -1)
    return lax.all_to_all(split, TEAM, 0, 0, tiled=True).reshape(team * tokens, -1)


def own_rows(value):
    ny, nc, nzh = lax.axis_size("y"), lax.axis_size("core"), lax.axis_size("zh")
    split = value.reshape(value.shape[0], ny, nc, nzh, lax.axis_size(CHIPS), -1)
    split = lax.dynamic_index_in_dim(split, lax.axis_index("core"), 2, keepdims=False)
    split = lax.dynamic_index_in_dim(split, lax.axis_index(CHIPS), 3, keepdims=False)
    return split.reshape(value.shape[0], -1)


def sum_over(value, axes):
    for axis in axes:
        k = 1
        while k < lax.axis_size(axis):
            value = value + swap(value, axis, k)
            k *= 2
    return value


def local(
    layer_input,
    segments,
    positions,
    query_key_value_weight,
    w_out,
    w_gate,
    w_up,
    w_down,
    g_attn,
    g_ffn,
    g_query,
    g_key,
    cotangent,
):
    tokens, model = layer_input.shape
    back = lax.axis_size(SEQ) // 2
    ff = w_gate.shape[1] // lax.axis_size(TEAM)

    inputs = layer_input.astype(f32)
    scale_in = row_scale(inputs)
    normed_in = inputs * scale_in
    normed_low = (normed_in * g_attn).astype(bf16)

    team = lax.axis_size(TEAM)
    joined_columns = query_key_value_weight.shape[1]
    padded = -(-joined_columns // (128 * team)) * 128 * team

    y, zh = lax.axis_index("y"), lax.axis_index("zh")
    ny, nc, nzh = lax.axis_size("y"), lax.axis_size("core"), lax.axis_size("zh")
    width = model // (ny * nc * nzh)
    offsets = jnp.stack(
        [
            (((y ^ a) * nc + c) * nzh + (zh ^ b)) * width
            for b in range(nzh)
            for a in range(ny)
            for c in range(nc)
        ]
    ).astype(jnp.int32)

    normed_team = lax.all_gather(normed_low, TEAM, axis=0, tiled=True)
    qkv_block = team_columns([jnp.pad(query_key_value_weight, ((0, 0), (0, padded - joined_columns)))])
    qkv_block, w_down, w_out = tie(qkv_block, w_down, w_out)
    qkv_near, qkv_far = exchange(qkv_block, "y"), exchange(qkv_block, "zh")
    out_near = exchange(w_out[None, None], "zh")
    down_block = team_columns([w_down])
    out_part = [exchange(piece, "y") for piece in out_near]
    qkv_part = place([qkv_near] + [exchange(piece, "y") for piece in qkv_far[1:]])
    out_rows = jnp.zeros((ny, nzh) + w_out.shape, bf16)
    for b, row in enumerate(out_part):
        for a, piece in enumerate(row):
            out_rows = lax.dynamic_update_slice(out_rows, piece, (y ^ a, zh ^ b, 0, 0))

    normed_team, qkv_part, out_rows, down_block, w_gate = tie(
        normed_team, qkv_part, out_rows, down_block, w_gate
    )
    out_full = lax.all_gather(out_rows, TEAM, axis=0, tiled=False)
    out_full = (
        out_full.reshape((nc, lax.axis_size(CHIPS)) + out_rows.shape)
        .transpose(2, 0, 3, 1, 4, 5)
        .reshape(model, -1)
    )
    down_far, down_near = exchange(down_block, "zh"), exchange(down_block, "y")
    joined_team = dot_nn(normed_team, qkv_part).astype(bf16)
    joined = lax.all_to_all(
        joined_team.reshape(team, tokens, -1), TEAM, 0, 0, tiled=True
    )
    joined, w_gate, w_up, down_near = tie(joined, w_gate, w_up, down_near)
    gate_up_block = team_columns([w_gate, w_up])

    half = HEAD_DIM // 2
    frequency = 10000.0 ** (-jnp.arange(half, dtype=f32) / half)
    angles = positions.astype(f32)[:, None] * frequency[None, :]
    angles = jnp.concatenate([angles, angles], axis=-1)
    cosine, sine = jnp.cos(angles), jnp.sin(angles)
    gq, gk = g_query[None, :], g_key[None, :]
    query_low, kv_low = whole(
        heads_forward_kernel,
        (
            jax.ShapeDtypeStruct((tokens, QUERY_COLUMNS), bf16),
            jax.ShapeDtypeStruct((tokens, 2 * KEY_COLUMNS), bf16),
        ),
        "heads_forward",
        tokens * 1920 * 20,
        tokens * 1920 * 6,
    )(joined, cosine, sine, gq, gk)

    kv_blocks = [kv_low] + [shifted(kv_low, step) for step in range(1, back + 1)]
    kv_blocks, down_far, gate_up_block, cotangent_in = tie(
        kv_blocks, down_far, gate_up_block, cotangent
    )
    gate_block, up_block = gate_up_block[..., :ff], gate_up_block[..., ff:]
    gate_far = exchange(gate_block, "zh")
    grads_out = lax.all_gather(cotangent_in, TEAM, axis=0, tiled=True)
    tiled_positions = jnp.tile(positions[None, :], (1, GROUP))
    attended, inverse = whole(
        functools.partial(attend_forward_kernel, back),
        (
            jax.ShapeDtypeStruct((tokens, QUERY_COLUMNS), bf16),
            jax.ShapeDtypeStruct((8, GROUP * tokens), f32),
        ),
        "attend_forward",
        4 * tokens * tokens * (back + 1) * QUERY_COLUMNS,
        tokens * 2000 * 10,
    )(tiled_positions, query_low, *kv_blocks)

    gate_near = exchange(gate_block, "y")
    down_blocks = down_near + sum([exchange(piece, "y") for piece in down_far[1:]], [])
    attended, out_full, gate_far, up_block, gate_near = tie(
        attended, out_full, gate_far, up_block, gate_near
    )
    up_far, up_near = exchange(up_block, "zh"), exchange(up_block, "y")
    gate_blocks = gate_near + sum([exchange(piece, "y") for piece in gate_far[1:]], [])
    middle = inputs + dot_nt(attended, out_full)
    scale_mid = row_scale(middle)
    normed_mid = middle * scale_mid
    mid_low = (normed_mid * g_ffn).astype(bf16)
    mid_team = lax.all_gather(mid_low, TEAM, axis=0, tiled=True)

    products = 2 * mid_team.shape[0] * model * ff
    up_blocks = up_near + sum([exchange(piece, "y") for piece in up_far[1:]], [])
    (hidden_grad,) = by_tokens(
        ffn_dz_kernel, offsets, [grads_out], down_blocks, [(ff, f32)], "ffn_dz", products
    )
    hidden_grad, gate_blocks, up_blocks = tie(hidden_grad, gate_blocks, up_blocks)
    mid_team, hidden_grad, attended_in = tie(mid_team, hidden_grad, attended)
    attended_team = lax.all_gather(attended_in, TEAM, axis=0, tiled=True)
    hidden, gate_grad, up_grad, mid_part = by_tokens(
        ffn_mid_kernel,
        offsets,
        [mid_team, hidden_grad],
        gate_blocks + up_blocks,
        [(ff, bf16), (ff, bf16), (ff, bf16), (model, bf16)],
        "ffn_mid",
        4 * products,
    )

    scatter = lambda part: lax.psum_scatter(part, ("y", "zh"), scatter_dimension=0, tiled=True)
    mid_part, attended_team, hidden = tie(mid_part, attended_team, hidden)
    mid_half = team_core(mid_part)
    down_part = weight_grad(grads_out, hidden, "down_grad")
    down_sum = scatter(down_part)
    mid_half, hidden, _ = tie(mid_half, hidden, down_part)
    mid_grad = team_chips(mid_half)
    branch_half = team_core(
        by_tokens(
            ffn_out_kernel, offsets, [hidden], down_blocks, [(model, bf16)], "ffn_out", products
        )[0]
    )
    mid_grad, branch_half, mid_team, gate_grad, up_grad = tie(
        mid_grad, branch_half, mid_team, gate_grad, up_grad
    )

    weighted = mid_grad * g_ffn
    ffn_gain = jnp.sum(mid_grad * normed_mid, axis=0)
    middle_grad = cotangent.astype(f32) + scale_mid * (
        weighted - normed_mid * jnp.mean(weighted * normed_mid, axis=-1, keepdims=True)
    )
    branch_grad = middle_grad.astype(bf16)
    head_grads = dot_nn(branch_grad, out_full).astype(bf16)
    results = whole(
        functools.partial(attend_backward_kernel, back),
        (
            jax.ShapeDtypeStruct((tokens, QUERY_COLUMNS), f32),
            jax.ShapeDtypeStruct((tokens, 2 * KEY_COLUMNS), f32),
        )
        + (jax.ShapeDtypeStruct((tokens, 2 * KEY_COLUMNS), bf16),) * back,
        "attend_backward",
        10 * tokens * tokens * (back + 1) * QUERY_COLUMNS,
        tokens * 2000 * 20,
    )(tiled_positions, query_low, head_grads, inverse, *kv_blocks)
    query_grad, own_grad, far_grads = results[0], results[1], results[2:]
    far_grads, gate_grad, mid_team_in = tie(far_grads, gate_grad, mid_team)
    gate_part = weight_grad(mid_team_in, gate_grad, "gate_grad")
    received = [shifted(grad, -(i + 1)) for i, grad in enumerate(far_grads)]
    received, down_sum, gate_part, up_grad = tie(received, down_sum, gate_part, up_grad)
    gate_sum = scatter(gate_part)
    joined_grad, head_gains = whole(
        functools.partial(heads_backward_kernel, back),
        (
            jax.ShapeDtypeStruct(joined.shape, bf16),
            jax.ShapeDtypeStruct((1, 2 * HEAD_DIM), f32),
        ),
        "heads_backward",
        tokens * 1920 * 30,
        tokens * 1920 * 16,
    )(joined, cosine, sine, gq, gk, query_grad, own_grad, *received)

    joined_grad, up_grad, mid_team = tie(joined_grad, up_grad, mid_team)
    up_part = weight_grad(mid_team, up_grad, "up_grad")
    joined_grad = lax.all_to_all(joined_grad, TEAM, 0, 0, tiled=True).reshape(-1, padded // team)
    joined_grad, up_part, down_sum = tie(joined_grad, up_part, down_sum)
    up_sum = scatter(up_part)
    normed_half = team_core(dot_nt(joined_grad, qkv_part).astype(bf16))
    normed_half, branch_grad = tie(normed_half, branch_grad)
    normed_in_grad = team_chips(normed_half)
    branch_rows = row_team(branch_grad)
    normed_in_grad, gate_sum, joined_grad, down_sum, branch_rows, branch_half = tie(
        normed_in_grad, gate_sum, joined_grad, down_sum, branch_rows, branch_half
    )
    qkv_sum = reduce_zh(
        reduce_y(
            dot_tn(normed_team, joined_grad).astype(bf16).reshape(ny, nc, nzh, -1, padded // team)
        )
    )
    w_down_grad, w_gate_grad = return_columns([down_sum, gate_sum])
    out_part = dot_tn(branch_rows, attended_team).astype(bf16)
    out_sum = reduce_y(out_part.reshape(ny, 1, nzh, -1, out_part.shape[1]))
    branch_two = team_chips(branch_half)
    weighted_in = normed_in_grad * g_attn
    attn_gain = jnp.sum(normed_in_grad * normed_in, axis=0)
    input_grad = (
        middle_grad
        + scale_in
        * (weighted_in - normed_in * jnp.mean(weighted_in * normed_in, axis=-1, keepdims=True))
    ).astype(bf16)

    gains = sum_over(
        jnp.concatenate([attn_gain, ffn_gain, head_gains[0]], axis=0).reshape(-1, 128),
        ("core", "x"),
    )
    gains, up_sum, qkv_sum, out_sum, branch_two = tie(
        gains, up_sum, qkv_sum, out_sum, branch_two
    )
    w_up_grad, w_qkv_grad = return_columns([up_sum, qkv_sum])
    w_qkv_grad = w_qkv_grad[:, :joined_columns]
    gains = sum_over(gains, ("y", "zl", "zh")).reshape(-1)
    w_out_grad = reduce_zh(out_sum).reshape(-1, out_sum.shape[-1])
    result = (middle + branch_two).astype(bf16)
    return (
        result,
        input_grad,
        w_qkv_grad,
        w_out_grad,
        w_gate_grad,
        w_up_grad,
        w_down_grad,
        gains[:model],
        gains[model : 2 * model],
        gains[2 * model : 2 * model + HEAD_DIM],
        gains[2 * model + HEAD_DIM :],
    )


def solution(mesh):
    inner, outer = mesh.devices.shape
    split = Mesh(mesh.devices.reshape(inner // 2, 2, 2, 2, outer // 4), ALL)
    rows, whole_array = P(ALL, None), P()
    in_specs = (rows, P(ALL), P(ALL)) + (rows,) * 5 + (whole_array,) * 4 + (rows,)
    out_specs = (rows,) * 7 + (whole_array,) * 4
    return jax.shard_map(local, mesh=split, in_specs=in_specs, out_specs=out_specs, check_vma=False)
```
